128 devices in a mesh: gx: 4 (over y), gy: 8 (over x, core), gz: 4 (over z).
Axes of the slice: x: 4, y: 4, z: 4, core: 2. Of those that a mesh axis runs over, the one named last changes fastest.
Arguments:
- volume: bfloat16 [48, 64, 65536], P(None, 'gz', ('gx', 'gy')), may hold values from -6 to 6
- tissue: int32 [32, 32, 4], replicated, may hold values 0 or 1
- w_down1: bfloat16 [8, 64, 48], replicated, may hold values from -0.4375 to 0.4375
- b_down1: float32 [64], replicated, may hold values from -1.5 to 1.5
- w_conv1a: bfloat16 [27, 64, 64], replicated, may hold values from -0.21875 to 0.21875
- b_conv1a: float32 [64], replicated, may hold values from -1.5 to 1.5
- w_conv1b: bfloat16 [27, 64, 64], replicated, may hold values from -0.21875 to 0.21875
- b_conv1b: float32 [64], replicated, may hold values from -1.5 to 1.5
- w_down2: bfloat16 [8, 96, 64], replicated, may hold values from -0.375 to 0.375
- b_down2: float32 [96], replicated, may hold values from -1.5 to 1.5
- w_conv2a: bfloat16 [27, 96, 96], replicated, may hold values from -0.15625 to 0.15625
- b_conv2a: float32 [96], replicated, may hold values from -1.5 to 1.5
- w_conv2b: bfloat16 [27, 96, 96], replicated, may hold values from -0.15625 to 0.15625
- b_conv2b: float32 [96], replicated, may hold values from -1.5 to 1.5
Outputs:
- level_one: bfloat16 [64, 32, 16384], P(None, 'gz', ('gx', 'gy'))
- level_two: bfloat16 [96, 16, 4096], P(None, 'gz', ('gx', 'gy'))
The draws below stay inside these ranges and needn't reach their ends.
All inputs are finite; a program needn't handle non-finite values.
Results may differ from the reference program's by a relative error of at most 0.012.
Values may be sent and summed in bfloat16 or wider, within the bound.
A program may use at most 128 MiB of HBM per device.

```python
import jax
import jax.numpy as jnp
from jax import lax

C0 = 48
C1 = 64
C2 = 96
CX = 64
CY = 32
NX = 256
NY = 256
NZ = 64
N_GX = 4
N_GY = 8


def with_ends(values, key, low, largest):
    longest = values.shape.index(max(values.shape))
    spots = []
    for shift in (0, 1):
        where = [jax.random.randint(jax.random.fold_in(key, axis), (), 0, length) for axis, length in enumerate(values.shape)]
        where[longest] = (where[longest] + shift) % values.shape[longest]
        spots.append(tuple(where))
    return values.at[spots[0]].set(low).at[spots[1]].set(largest)


def block_levels(stream_key, shape, shards, low, top_value):
    def one(position, blocks):
        draws = jax.random.uniform(jax.random.fold_in(jax.random.fold_in(stream_key, 6), position), (blocks,), jnp.float32, low / len(shards), top_value / len(shards))
        return jnp.repeat(jnp.exp(draws), shape[position] // blocks).reshape((-1,) + (1,) * (len(shape) - position - 1))

    level = one(*shards[0])
    for cut in shards[1:]:
        level = level * one(*cut)
    return level


def normal_values(stream_key, dims, deviation, reach, cuts=(), kind=jnp.bfloat16):
    factor_of = block_levels(stream_key, dims, cuts, -0.22, 0.18) if cuts else 1.0
    array = jax.random.normal(stream_key, dims, jnp.float32) * deviation * factor_of
    return jnp.minimum(jnp.maximum(array, -reach), reach).astype(kind)


def setup_inputs(seed: int = 0) -> dict:
    keys = jax.random.split(jax.random.key(seed), 15)
    volume = normal_values(keys[0], (C0, NZ, NX * NY), 1.0, 6.0, ((1, 4), (2, 32)))
    tissue = with_ends((jax.random.randint(keys[1], (NX // 8, NY // 8, NZ // 16), 0, 3) < 2).astype(jnp.int32), jax.random.fold_in(keys[1], 1), 0, 1)
    w_down1 = normal_values(keys[2], (8, C1, C0), (C0 * 4) ** -0.5, 0.4375)
    b_down1 = normal_values(keys[3], (C1,), 0.3, 1.5, (), jnp.float32)
    w_conv1a = normal_values(keys[4], (27, C1, C1), (C1 * 27 // 2) ** -0.5, 0.21875)
    b_conv1a = normal_values(keys[5], (C1,), 0.3, 1.5, (), jnp.float32)
    w_conv1b = normal_values(keys[6], (27, C1, C1), (C1 * 27 // 2) ** -0.5, 0.21875)
    b_conv1b = normal_values(keys[7], (C1,), 0.3, 1.5, (), jnp.float32)
    w_down2 = normal_values(keys[8], (8, C2, C1), (C1 * 4) ** -0.5, 0.375)
    b_down2 = normal_values(keys[9], (C2,), 0.3, 1.5, (), jnp.float32)
    w_conv2a = normal_values(keys[10], (27, C2, C2), (C2 * 27 // 2) ** -0.5, 0.15625)
    b_conv2a = normal_values(keys[11], (C2,), 0.3, 1.5, (), jnp.float32)
    w_conv2b = normal_values(keys[12], (27, C2, C2), (C2 * 27 // 2) ** -0.5, 0.15625)
    b_conv2b = normal_values(keys[13], (C2,), 0.3, 1.5, (), jnp.float32)
    return dict(volume=volume, tissue=tissue, w_down1=w_down1, b_down1=b_down1, w_conv1a=w_conv1a, b_conv1a=b_conv1a, w_conv1b=w_conv1b, b_conv1b=b_conv1b, w_down2=w_down2, b_down2=b_down2, w_conv2a=w_conv2a, b_conv2a=b_conv2a, w_conv2b=w_conv2b, b_conv2b=b_conv2b)


def upsample(tissue, fx, fy, fz):
    grown = jnp.repeat(tissue.astype(jnp.float32), fx, axis=0)
    grown = jnp.repeat(grown, fy, axis=1)
    return jnp.repeat(grown, fz, axis=2)


def activate(summed, offsets, tissue_mask):
    return (jnp.maximum(summed + offsets[:, None, None, None], 0.0) * tissue_mask).astype(jnp.bfloat16)


def conv_same(field, weights):
    kernel = weights.astype(jnp.float32).reshape(3, 3, 3, weights.shape[1], weights.shape[2]).transpose(3, 4, 0, 1, 2)
    result = lax.conv_general_dilated(field.astype(jnp.float32)[None], kernel, (1, 1, 1), ((1, 1), (1, 1), (1, 1)),
                                      dimension_numbers=("NCDHW", "OIDHW", "NCDHW"), precision=lax.Precision.HIGHEST)
    return result[0]


def conv_down(field, weights):
    kernel = weights.astype(jnp.float32).reshape(2, 2, 2, weights.shape[1], weights.shape[2]).transpose(3, 4, 0, 1, 2)
    result = lax.conv_general_dilated(field.astype(jnp.float32)[None], kernel, (2, 2, 2), "VALID",
                                      dimension_numbers=("NCDHW", "OIDHW", "NCDHW"), precision=lax.Precision.HIGHEST)
    return result[0]


def unpack(packed, block_x, block_y):
    chans, depth = packed.shape[0], packed.shape[1]
    split = packed.reshape(chans, depth, N_GX, N_GY, block_y, block_x)
    return split.transpose(0, 2, 5, 3, 4, 1).reshape(chans, N_GX * block_x, N_GY * block_y, depth)


def pack(grid, block_x, block_y):
    chans, depth = grid.shape[0], grid.shape[3]
    split = grid.reshape(chans, N_GX, block_x, N_GY, block_y, depth)
    return split.transpose(0, 5, 1, 3, 4, 2).reshape(chans, depth, -1)


def reference(volume, tissue, w_down1, b_down1, w_conv1a, b_conv1a, w_conv1b, b_conv1b,
              w_down2, b_down2, w_conv2a, b_conv2a, w_conv2b, b_conv2b):
    grid_zero = unpack(volume, CX, CY)
    mask_one = upsample(tissue, 4, 4, 8)
    mask_two = upsample(tissue, 2, 2, 4)
    slab_count = 8
    slab_width = grid_zero.shape[1] // slab_count

    def one_slab(number):
        piece = lax.dynamic_slice_in_dim(grid_zero, number * slab_width, slab_width, 1)
        return conv_down(piece, w_down1)

    slab_terms = lax.map(one_slab, jnp.arange(slab_count, dtype=jnp.int32))
    summed = jnp.moveaxis(slab_terms, 0, 1).reshape(w_down1.shape[1], -1, slab_terms.shape[3], slab_terms.shape[4])
    down_one = activate(summed, b_down1, mask_one)
    inner_one = activate(conv_same(down_one, w_conv1a), b_conv1a, mask_one)
    feat_one = activate(conv_same(inner_one, w_conv1b), b_conv1b, mask_one)
    down_two = activate(conv_down(feat_one, w_down2), b_down2, mask_two)
    inner_two = activate(conv_same(down_two, w_conv2a), b_conv2a, mask_two)
    feat_two = activate(conv_same(inner_two, w_conv2b), b_conv2b, mask_two)
    return (pack(feat_one, CX // 2, CY // 2), pack(feat_two, CX // 4, CY // 4))
```

```python
import jax
import jax.numpy as jnp
from jax import lax
from jax.sharding import PartitionSpec as P

CX = 64
CY = 32


def padded_2(cells, sides, width):
    for axis, dim in sides:
        count = lax.axis_size(axis)
        ends = count - 1
        head = lax.slice_in_dim(cells, 0, width, axis=dim)
        tail = lax.slice_in_dim(cells, cells.shape[dim] - width, cells.shape[dim], axis=dim)
        cells = jnp.concatenate(
            [
                lax.ppermute(tail, axis, [(i, (i + 1) % count) for i in range(ends)]),
                cells,
                lax.ppermute(head, axis, [((i + 1) % count, i) for i in range(ends)]),
            ],
            axis=dim,
        )
    return cells


def region_mask(tissue, repeats, block_starts, extents, margin):
    padded = jnp.pad(tissue, 1)
    counts = [extents[d] // repeats[d] + 2 for d in range(3)]
    starts = [jnp.asarray(block_starts[d], dtype=jnp.int32) for d in range(3)]
    table = lax.dynamic_slice(padded, starts, counts)
    for d in range(3):
        table = jnp.repeat(table, repeats[d], axis=d)
    table = table[
        repeats[0] - margin : repeats[0] + extents[0] + margin,
        repeats[1] - margin : repeats[1] + extents[1] + margin,
        repeats[2] - margin : repeats[2] + extents[2] + margin,
    ]
    return table.astype(jnp.float32).transpose(2, 1, 0)


def finish(summed, offsets, tissue_mask):
    return (jnp.maximum(summed + offsets[:, None, None, None], 0.0) * tissue_mask).astype(
        jnp.bfloat16
    )


def conv_taps(padded, weights):
    kernel = weights.reshape(3, 3, 3, weights.shape[1], weights.shape[2]).transpose(3, 4, 2, 1, 0)
    result = lax.conv_general_dilated(
        padded[None], kernel, (1, 1, 1), "VALID",
        dimension_numbers=("NCDHW", "OIDHW", "NCDHW"), preferred_element_type=jnp.float32)
    return result[0]


def down_taps(field, weights):
    kernel = weights.reshape(2, 2, 2, weights.shape[1], weights.shape[2]).transpose(3, 4, 2, 1, 0)
    result = lax.conv_general_dilated(
        field[None], kernel, (2, 2, 2), "VALID",
        dimension_numbers=("NCDHW", "OIDHW", "NCDHW"), preferred_element_type=jnp.float32)
    return result[0]


def flatten_cells(field):
    return field.reshape(field.shape[0], field.shape[1], field.shape[2] * field.shape[3])


def local(volume, tissue, w_down1, b_down1, w_conv1a, b_conv1a, w_conv1b, b_conv1b,
          w_down2, b_down2, w_conv2a, b_conv2a, w_conv2b, b_conv2b):
    index_x = lax.axis_index("gx")
    index_y = lax.axis_index("gy")
    index_z = lax.axis_index("gz")
    grid_zero = volume.reshape(volume.shape[0], volume.shape[1], CY, CX)
    first_x = CX // 2
    first_y = CY // 2
    first_z = volume.shape[1] // 2
    first_blocks = (index_x * (first_x // 4), index_y * (first_y // 4), index_z * (first_z // 8))
    mask_one = region_mask(tissue, (4, 4, 8), first_blocks, (first_x, first_y, first_z), 0)
    mask_one_wide = region_mask(tissue, (4, 4, 8), first_blocks, (first_x, first_y, first_z), 1)
    down_one = finish(down_taps(grid_zero, w_down1), b_down1, mask_one)
    sides = (("gx", 3), ("gy", 2), ("gz", 1))
    inner_one = finish(conv_taps(padded_2(down_one, sides, 2), w_conv1a), b_conv1a, mask_one_wide)
    feat_one = finish(conv_taps(inner_one, w_conv1b), b_conv1b, mask_one)
    second_x = first_x // 2
    second_y = first_y // 2
    second_z = first_z // 2
    second_blocks = (index_x * (second_x // 2), index_y * (second_y // 2), index_z * (second_z // 4))
    mask_two = region_mask(tissue, (2, 2, 4), second_blocks, (second_x, second_y, second_z), 0)
    mask_two_wide = region_mask(tissue, (2, 2, 4), second_blocks, (second_x, second_y, second_z), 1)
    down_two = finish(down_taps(feat_one, w_down2), b_down2, mask_two)
    middle = finish(conv_taps(padded_2(down_two, sides, 2), w_conv2a), b_conv2a, mask_two_wide)
    feat_two = finish(conv_taps(middle, w_conv2b), b_conv2b, mask_two)
    return (flatten_cells(feat_one), flatten_cells(feat_two))


def solution(mesh):
    return jax.shard_map(
        local,
        mesh=mesh,
        in_specs=(P(None, "gz", ("gx", "gy")),) + (P(),) * 13,
        out_specs=(P(None, "gz", ("gx", "gy")), P(None, "gz", ("gx", "gy"))),
        check_vma=False,
    )
```

```python
import functools

import jax
import jax.numpy as jnp
from jax import lax
from jax.experimental import pallas as pl
from jax.experimental.pallas import tpu as pltpu
from jax.sharding import PartitionSpec as P

CX = 64
CY = 32
AXES = ("gx", "gy", "gz")
MESH = pl.DeviceIdType.MESH
DIRS = [
    (dx, dy, dz)
    for dx in (-1, 0, 1)
    for dy in (-1, 0, 1)
    for dz in (-1, 0, 1)
    if (dx, dy, dz) != (0, 0, 0)
]


def rim_kernel(width, f_ref, p_ref, local_sem, send_sem, recv_sem):
    size_z, size_y, size_x, _ = f_ref.shape
    sizes = (size_x, size_y, size_z)
    index = [lax.axis_index(a) for a in AXES]
    count = [lax.axis_size(a) for a in AXES]

    def exists(d):
        ok = True
        for a in range(3):
            if d[a] == -1:
                ok = jnp.logical_and(ok, index[a] > 0)
            elif d[a] == 1:
                ok = jnp.logical_and(ok, index[a] < count[a] - 1)
        return ok

    def device(d):
        return tuple(index[a] + d[a] for a in range(3))

    def source(a, step):
        s = sizes[a]
        if step == -1:
            return slice(0, width)
        if step == 1:
            return slice(s - width, s)
        return slice(0, s)

    def side(a, step):
        s = sizes[a]
        if step == -1:
            return slice(0, width)
        if step == 1:
            return slice(s + width, s + 2 * width)
        return slice(width, width + s)

    barrier = pltpu.get_barrier_semaphore()
    for d in DIRS:
        @pl.when(exists(d))
        def _():
            pl.semaphore_signal(barrier, inc=1, device_id=device(d), device_id_type=MESH)

    local = pltpu.make_async_copy(
        f_ref, p_ref.at[width:width + size_z, width:width + size_y, width:width + size_x, :],
        local_sem.at[0])
    local.start()

    for d in DIRS:
        @pl.when(jnp.logical_not(exists(d)))
        def _():
            sx, sy, sz = (side(a, d[a]) for a in range(3))
            region = p_ref.at[sz, sy, sx, :]
            region[...] = jnp.zeros(region.shape, region.dtype)

    peers = 1
    for a in range(3):
        below = (index[a] + count[a] - 1) // count[a]
        above = (2 * count[a] - 2 - index[a]) // count[a]
        peers = peers * (1 + below + above)
    pl.semaphore_wait(barrier, peers - 1)

    copies = []
    for k, d in enumerate(DIRS):
        sx, sy, sz = (source(a, d[a]) for a in range(3))
        tx, ty, tz = (side(a, -d[a]) for a in range(3))
        copy = pltpu.make_async_remote_copy(
            src_ref=f_ref.at[sz, sy, sx, :],
            dst_ref=p_ref.at[tz, ty, tx, :],
            send_sem=send_sem.at[k],
            recv_sem=recv_sem.at[k],
            device_id=device(d),
            device_id_type=MESH,
        )
        copies.append((d, copy))

        @pl.when(exists(d))
        def _():
            copy.start()

    local.wait()
    for d, copy in copies:
        @pl.when(exists(d))
        def _():
            copy.wait_send()

        @pl.when(exists(tuple(-v for v in d)))
        def _():
            copy.wait_recv()


def with_rim(field, width, collective_id):
    size_z, size_y, size_x, chans = field.shape
    return pl.pallas_call(
        functools.partial(rim_kernel, width),
        out_shape=jax.ShapeDtypeStruct(
            (size_z + 2 * width, size_y + 2 * width, size_x + 2 * width, chans), field.dtype),
        in_specs=[pl.BlockSpec(memory_space=pltpu.VMEM)],
        out_specs=pl.BlockSpec(memory_space=pltpu.VMEM),
        scratch_shapes=[
            pltpu.SemaphoreType.DMA((1,)),
            pltpu.SemaphoreType.DMA((len(DIRS),)),
            pltpu.SemaphoreType.DMA((len(DIRS),)),
        ],
        compiler_params=pltpu.CompilerParams(collective_id=collective_id, has_side_effects=True),
    )(field)


def region_mask(tissue, repeats, block_starts, extents, margin):
    padded = jnp.pad(tissue, 1)
    counts = [extents[d] // repeats[d] + 2 for d in range(3)]
    starts = [jnp.asarray(block_starts[d], dtype=jnp.int32) for d in range(3)]
    table = lax.dynamic_slice(padded, starts, counts)
    for d in range(3):
        table = jnp.repeat(table, repeats[d], axis=d)
    table = table[
        repeats[0] - margin : repeats[0] + extents[0] + margin,
        repeats[1] - margin : repeats[1] + extents[1] + margin,
        repeats[2] - margin : repeats[2] + extents[2] + margin,
    ]
    return table.astype(jnp.float32).transpose(2, 1, 0)[..., None]


def finish(summed, offsets, tissue_mask):
    return (jnp.maximum(summed + offsets, 0.0) * tissue_mask).astype(jnp.bfloat16)


def conv_taps(padded, weights):
    kernel = weights.reshape(3, 3, 3, weights.shape[1], weights.shape[2]).transpose(2, 1, 0, 4, 3)
    result = lax.conv_general_dilated(
        padded[None], kernel, (1, 1, 1), "VALID",
        dimension_numbers=("NDHWC", "DHWIO", "NDHWC"), preferred_element_type=jnp.float32)
    return result[0]


def down_first(grid, weights):
    kernel = weights.reshape(2, 2, 2, weights.shape[1], weights.shape[2]).transpose(2, 1, 0, 4, 3)
    result = lax.conv_general_dilated(
        grid[None], kernel, (2, 2, 2), "VALID",
        dimension_numbers=("NCDHW", "DHWIO", "NDHWC"), preferred_element_type=jnp.float32)
    return result[0]


def down_cells(field, weights):
    kernel = weights.reshape(2, 2, 2, weights.shape[1], weights.shape[2]).transpose(2, 1, 0, 4, 3)
    result = lax.conv_general_dilated(
        field[None], kernel, (2, 2, 2), "VALID",
        dimension_numbers=("NDHWC", "DHWIO", "NDHWC"), preferred_element_type=jnp.float32)
    return result[0]


def packed(field):
    size_z, size_y, size_x, chans = field.shape
    return field.transpose(3, 0, 1, 2).reshape(chans, size_z, size_y * size_x)


def local(volume, tissue, w_down1, b_down1, w_conv1a, b_conv1a, w_conv1b, b_conv1b,
          w_down2, b_down2, w_conv2a, b_conv2a, w_conv2b, b_conv2b):
    index_x = lax.axis_index("gx")
    index_y = lax.axis_index("gy")
    index_z = lax.axis_index("gz")
    grid_zero = volume.reshape(volume.shape[0], volume.shape[1], CY, CX)
    first_x = CX // 2
    first_y = CY // 2
    first_z = volume.shape[1] // 2
    first_blocks = (index_x * (first_x // 4), index_y * (first_y // 4), index_z * (first_z // 8))
    mask_one = region_mask(tissue, (4, 4, 8), first_blocks, (first_x, first_y, first_z), 0)
    mask_one_wide = region_mask(tissue, (4, 4, 8), first_blocks, (first_x, first_y, first_z), 1)
    down_one = finish(down_first(grid_zero, w_down1), b_down1, mask_one)
    inner_one = finish(conv_taps(with_rim(down_one, 2, 0), w_conv1a), b_conv1a, mask_one_wide)
    feat_one = finish(conv_taps(inner_one, w_conv1b), b_conv1b, mask_one)
    second_x = first_x // 2
    second_y = first_y // 2
    second_z = first_z // 2
    second_blocks = (index_x * (second_x // 2), index_y * (second_y // 2), index_z * (second_z // 4))
    mask_two = region_mask(tissue, (2, 2, 4), second_blocks, (second_x, second_y, second_z), 0)
    mask_two_wide = region_mask(tissue, (2, 2, 4), second_blocks, (second_x, second_y, second_z), 1)
    down_two = finish(down_cells(feat_one, w_down2), b_down2, mask_two)
    middle = finish(conv_taps(with_rim(down_two, 2, 1), w_conv2a), b_conv2a, mask_two_wide)
    feat_two = finish(conv_taps(middle, w_conv2b), b_conv2b, mask_two)
    return (packed(feat_one), packed(feat_two))


def solution(mesh):
    return jax.shard_map(
        local,
        mesh=mesh,
        in_specs=(P(None, "gz", ("gx", "gy")),) + (P(),) * 13,
        out_specs=(P(None, "gz", ("gx", "gy")), P(None, "gz", ("gx", "gy"))),
        check_vma=False,
    )
```

```python
import functools

import jax
import jax.numpy as jnp
from jax import lax
from jax.experimental import pallas as pl
from jax.experimental.pallas import tpu as pltpu
from jax.sharding import PartitionSpec as P

CX = 64
CY = 32
AXES = ("gx", "gy", "gz")
MESH = pl.DeviceIdType.MESH
DIRS = [
    (dx, dy, dz)
    for dx in (-1, 0, 1)
    for dy in (-1, 0, 1)
    for dz in (-1, 0, 1)
    if (dx, dy, dz) != (0, 0, 0)
]


def rim_kernel(width, f_ref, p_ref, local_sem, send_sem, recv_sem):
    size_z, size_y, size_x, _ = f_ref.shape
    sizes = (size_x, size_y, size_z)
    index = [lax.axis_index(a) for a in AXES]
    count = [lax.axis_size(a) for a in AXES]

    def exists(d):
        ok = True
        for a in range(3):
            if d[a] == -1:
                ok = jnp.logical_and(ok, index[a] > 0)
            elif d[a] == 1:
                ok = jnp.logical_and(ok, index[a] < count[a] - 1)
        return ok

    def device(d):
        return tuple(index[a] + d[a] for a in range(3))

    def source(a, step):
        s = sizes[a]
        if step == -1:
            return slice(0, width)
        if step == 1:
            return slice(s - width, s)
        return slice(0, s)

    def side(a, step):
        s = sizes[a]
        if step == -1:
            return slice(0, width)
        if step == 1:
            return slice(s + width, s + 2 * width)
        return slice(width, width + s)

    barrier = pltpu.get_barrier_semaphore()
    for d in DIRS:
        @pl.when(exists(d))
        def _():
            pl.semaphore_signal(barrier, inc=1, device_id=device(d), device_id_type=MESH)

    local = pltpu.make_async_copy(
        f_ref, p_ref.at[width:width + size_z, width:width + size_y, width:width + size_x, :],
        local_sem.at[0])
    local.start()

    for d in DIRS:
        @pl.when(jnp.logical_not(exists(d)))
        def _():
            sx, sy, sz = (side(a, d[a]) for a in range(3))
            region = p_ref.at[sz, sy, sx, :]
            region[...] = jnp.zeros(region.shape, region.dtype)

    peers = 1
    for a in range(3):
        below = (index[a] + count[a] - 1) // count[a]
        above = (2 * count[a] - 2 - index[a]) // count[a]
        peers = peers * (1 + below + above)
    pl.semaphore_wait(barrier, peers - 1)

    copies = []
    for k, d in enumerate(DIRS):
        sx, sy, sz = (source(a, d[a]) for a in range(3))
        tx, ty, tz = (side(a, -d[a]) for a in range(3))
        copy = pltpu.make_async_remote_copy(
            src_ref=f_ref.at[sz, sy, sx, :],
            dst_ref=p_ref.at[tz, ty, tx, :],
            send_sem=send_sem.at[k],
            recv_sem=recv_sem.at[k],
            device_id=device(d),
            device_id_type=MESH,
        )
        copies.append((d, copy))

        @pl.when(exists(d))
        def _():
            copy.start()

    local.wait()
    for d, copy in copies:
        @pl.when(exists(d))
        def _():
            copy.wait_send()

        @pl.when(exists(tuple(-v for v in d)))
        def _():
            copy.wait_recv()


def with_rim(field, width, collective_id):
    size_z, size_y, size_x, chans = field.shape
    return pl.pallas_call(
        functools.partial(rim_kernel, width),
        out_shape=jax.ShapeDtypeStruct(
            (size_z + 2 * width, size_y + 2 * width, size_x + 2 * width, chans), field.dtype),
        in_specs=[pl.BlockSpec(memory_space=pltpu.VMEM)],
        out_specs=pl.BlockSpec(memory_space=pltpu.VMEM),
        scratch_shapes=[
            pltpu.SemaphoreType.DMA((1,)),
            pltpu.SemaphoreType.DMA((len(DIRS),)),
            pltpu.SemaphoreType.DMA((len(DIRS),)),
        ],
        compiler_params=pltpu.CompilerParams(collective_id=collective_id, has_side_effects=True),
    )(field)


def rim_cells(field, width, collective_id):
    rimmed = with_rim(field.transpose(1, 2, 3, 0), width, collective_id)
    return rimmed.transpose(3, 0, 1, 2)


def region_mask(tissue, repeats, block_starts, extents, margin):
    padded = jnp.pad(tissue, 1)
    counts = [extents[d] // repeats[d] + 2 for d in range(3)]
    starts = [jnp.asarray(block_starts[d], dtype=jnp.int32) for d in range(3)]
    table = lax.dynamic_slice(padded, starts, counts)
    for d in range(3):
        table = jnp.repeat(table, repeats[d], axis=d)
    table = table[
        repeats[0] - margin : repeats[0] + extents[0] + margin,
        repeats[1] - margin : repeats[1] + extents[1] + margin,
        repeats[2] - margin : repeats[2] + extents[2] + margin,
    ]
    return table.astype(jnp.float32).transpose(2, 1, 0)


def finish(summed, offsets, tissue_mask):
    return (jnp.maximum(summed + offsets[:, None, None, None], 0.0) * tissue_mask).astype(
        jnp.bfloat16
    )


def conv_taps(padded, weights):
    kernel = weights.reshape(3, 3, 3, weights.shape[1], weights.shape[2]).transpose(3, 4, 2, 1, 0)
    result = lax.conv_general_dilated(
        padded[None], kernel, (1, 1, 1), "VALID",
        dimension_numbers=("NCDHW", "OIDHW", "NCDHW"), preferred_element_type=jnp.float32)
    return result[0]


def down_taps(field, weights):
    kernel = weights.reshape(2, 2, 2, weights.shape[1], weights.shape[2]).transpose(3, 4, 2, 1, 0)
    result = lax.conv_general_dilated(
        field[None], kernel, (2, 2, 2), "VALID",
        dimension_numbers=("NCDHW", "OIDHW", "NCDHW"), preferred_element_type=jnp.float32)
    return result[0]


def flatten_cells(field):
    return field.reshape(field.shape[0], field.shape[1], field.shape[2] * field.shape[3])


def local(volume, tissue, w_down1, b_down1, w_conv1a, b_conv1a, w_conv1b, b_conv1b,
          w_down2, b_down2, w_conv2a, b_conv2a, w_conv2b, b_conv2b):
    index_x = lax.axis_index("gx")
    index_y = lax.axis_index("gy")
    index_z = lax.axis_index("gz")
    grid_zero = volume.reshape(volume.shape[0], volume.shape[1], CY, CX)
    first_x = CX // 2
    first_y = CY // 2
    first_z = volume.shape[1] // 2
    first_blocks = (index_x * (first_x // 4), index_y * (first_y // 4), index_z * (first_z // 8))
    mask_one = region_mask(tissue, (4, 4, 8), first_blocks, (first_x, first_y, first_z), 0)
    mask_one_wide = region_mask(tissue, (4, 4, 8), first_blocks, (first_x, first_y, first_z), 1)
    down_one = finish(down_taps(grid_zero, w_down1), b_down1, mask_one)
    inner_one = finish(conv_taps(rim_cells(down_one, 2, 0), w_conv1a), b_conv1a, mask_one_wide)
    feat_one = finish(conv_taps(inner_one, w_conv1b), b_conv1b, mask_one)
    second_x = first_x // 2
    second_y = first_y // 2
    second_z = first_z // 2
    second_blocks = (index_x * (second_x // 2), index_y * (second_y // 2), index_z * (second_z // 4))
    mask_two = region_mask(tissue, (2, 2, 4), second_blocks, (second_x, second_y, second_z), 0)
    mask_two_wide = region_mask(tissue, (2, 2, 4), second_blocks, (second_x, second_y, second_z), 1)
    down_two = finish(down_taps(feat_one, w_down2), b_down2, mask_two)
    middle = finish(conv_taps(rim_cells(down_two, 2, 1), w_conv2a), b_conv2a, mask_two_wide)
    feat_two = finish(conv_taps(middle, w_conv2b), b_conv2b, mask_two)
    return (flatten_cells(feat_one), flatten_cells(feat_two))


def solution(mesh):
    return jax.shard_map(
        local,
        mesh=mesh,
        in_specs=(P(None, "gz", ("gx", "gy")),) + (P(),) * 13,
        out_specs=(P(None, "gz", ("gx", "gy")), P(None, "gz", ("gx", "gy"))),
        check_vma=False,
    )
```

```python
import jax
import jax.numpy as jnp
from jax import lax
from jax.sharding import PartitionSpec as P

CX = 64
CY = 32


def padded_2(cells, sides, width):
    for axis, dim in sides:
        count = lax.axis_size(axis)
        ends = count - 1
        head = lax.slice_in_dim(cells, 0, width, axis=dim)
        tail = lax.slice_in_dim(cells, cells.shape[dim] - width, cells.shape[dim], axis=dim)
        cells = jnp.concatenate(
            [
                lax.ppermute(tail, axis, [(i, (i + 1) % count) for i in range(ends)]),
                cells,
                lax.ppermute(head, axis, [((i + 1) % count, i) for i in range(ends)]),
            ],
            axis=dim,
        )
    return cells


def region_mask(tissue, repeats, block_starts, extents, margin):
    padded = jnp.pad(tissue, 1)
    counts = [extents[d] // repeats[d] + 2 for d in range(3)]
    starts = [jnp.asarray(block_starts[d], dtype=jnp.int32) for d in range(3)]
    table = lax.dynamic_slice(padded, starts, counts)
    for d in range(3):
        table = jnp.repeat(table, repeats[d], axis=d)
    table = table[
        repeats[0] - margin : repeats[0] + extents[0] + margin,
        repeats[1] - margin : repeats[1] + extents[1] + margin,
        repeats[2] - margin : repeats[2] + extents[2] + margin,
    ]
    return table.astype(jnp.float32).transpose(2, 1, 0)


def finish(summed, offsets, tissue_mask):
    return (jnp.maximum(summed + offsets[:, None, None, None], 0.0) * tissue_mask).astype(
        jnp.bfloat16
    )


def conv_taps(padded, weights):
    kernel = weights.reshape(3, 3, 3, weights.shape[1], weights.shape[2]).transpose(3, 4, 2, 1, 0)
    result = lax.conv_general_dilated(
        padded[None], kernel, (1, 1, 1), "VALID",
        dimension_numbers=("NCDHW", "OIDHW", "NCDHW"), preferred_element_type=jnp.float32)
    return result[0]


def down_taps(field, weights):
    kernel = weights.reshape(2, 2, 2, weights.shape[1], weights.shape[2]).transpose(3, 4, 2, 1, 0)
    result = lax.conv_general_dilated(
        field[None], kernel, (2, 2, 2), "VALID",
        dimension_numbers=("NCDHW", "OIDHW", "NCDHW"), preferred_element_type=jnp.float32)
    return result[0]


def down_split(field, weights):
    channels, size_z, size_y, size_x = field.shape
    split = field.reshape(channels, size_z // 2, 2, size_y // 2, 2, size_x // 2, 2)
    grouped = weights.reshape(2, 2, 2, weights.shape[1], weights.shape[2])
    return jnp.einsum("abkoi,izkybxa->ozyx", grouped, split, preferred_element_type=jnp.float32)


def flatten_cells(field):
    return field.reshape(field.shape[0], field.shape[1], field.shape[2] * field.shape[3])


def local(volume, tissue, w_down1, b_down1, w_conv1a, b_conv1a, w_conv1b, b_conv1b,
          w_down2, b_down2, w_conv2a, b_conv2a, w_conv2b, b_conv2b):
    index_x = lax.axis_index("gx")
    index_y = lax.axis_index("gy")
    index_z = lax.axis_index("gz")
    grid_zero = volume.reshape(volume.shape[0], volume.shape[1], CY, CX)
    first_x = CX // 2
    first_y = CY // 2
    first_z = volume.shape[1] // 2
    first_blocks = (index_x * (first_x // 4), index_y * (first_y // 4), index_z * (first_z // 8))
    mask_one = region_mask(tissue, (4, 4, 8), first_blocks, (first_x, first_y, first_z), 0)
    mask_one_wide = region_mask(tissue, (4, 4, 8), first_blocks, (first_x, first_y, first_z), 1)
    down_one = finish(down_split(grid_zero, w_down1), b_down1, mask_one)
    sides = (("gx", 3), ("gy", 2), ("gz", 1))
    inner_one = finish(conv_taps(padded_2(down_one, sides, 2), w_conv1a), b_conv1a, mask_one_wide)
    feat_one = finish(conv_taps(inner_one, w_conv1b), b_conv1b, mask_one)
    second_x = first_x // 2
    second_y = first_y // 2
    second_z = first_z // 2
    second_blocks = (index_x * (second_x // 2), index_y * (second_y // 2), index_z * (second_z // 4))
    mask_two = region_mask(tissue, (2, 2, 4), second_blocks, (second_x, second_y, second_z), 0)
    mask_two_wide = region_mask(tissue, (2, 2, 4), second_blocks, (second_x, second_y, second_z), 1)
    down_two = finish(down_taps(feat_one, w_down2), b_down2, mask_two)
    middle = finish(conv_taps(padded_2(down_two, sides, 2), w_conv2a), b_conv2a, mask_two_wide)
    feat_two = finish(conv_taps(middle, w_conv2b), b_conv2b, mask_two)
    return (flatten_cells(feat_one), flatten_cells(feat_two))


def solution(mesh):
    return jax.shard_map(
        local,
        mesh=mesh,
        in_specs=(P(None, "gz", ("gx", "gy")),) + (P(),) * 13,
        out_specs=(P(None, "gz", ("gx", "gy")), P(None, "gz", ("gx", "gy"))),
        check_vma=False,
    )
```

```python
import functools

import jax
import jax.numpy as jnp
from jax import lax
from jax.experimental import pallas as pl
from jax.experimental.pallas import tpu as pltpu
from jax.sharding import PartitionSpec as P

CX = 64
CY = 32
AXES = ("gx", "gy", "gz")
MESH = pl.DeviceIdType.MESH
DIRS = [
    (dx, dy, dz)
    for dx in (-1, 0, 1)
    for dy in (-1, 0, 1)
    for dz in (-1, 0, 1)
    if (dx, dy, dz) != (0, 0, 0)
]


def rim_kernel(width, f_ref, p_ref, local_sem, send_sem, recv_sem):
    size_z, size_y, size_x, _ = f_ref.shape
    sizes = (size_x, size_y, size_z)
    index = [lax.axis_index(a) for a in AXES]
    count = [lax.axis_size(a) for a in AXES]

    def exists(d):
        ok = True
        for a in range(3):
            if d[a] == -1:
                ok = jnp.logical_and(ok, index[a] > 0)
            elif d[a] == 1:
                ok = jnp.logical_and(ok, index[a] < count[a] - 1)
        return ok

    def device(d):
        return tuple(index[a] + d[a] for a in range(3))

    def source(a, step):
        s = sizes[a]
        if step == -1:
            return slice(0, width)
        if step == 1:
            return slice(s - width, s)
        return slice(0, s)

    def side(a, step):
        s = sizes[a]
        if step == -1:
            return slice(0, width)
        if step == 1:
            return slice(s + width, s + 2 * width)
        return slice(width, width + s)

    barrier = pltpu.get_barrier_semaphore()
    for d in DIRS:
        @pl.when(exists(d))
        def _():
            pl.semaphore_signal(barrier, inc=1, device_id=device(d), device_id_type=MESH)

    local = pltpu.make_async_copy(
        f_ref, p_ref.at[width:width + size_z, width:width + size_y, width:width + size_x, :],
        local_sem.at[0])
    local.start()

    for d in DIRS:
        @pl.when(jnp.logical_not(exists(d)))
        def _():
            sx, sy, sz = (side(a, d[a]) for a in range(3))
            region = p_ref.at[sz, sy, sx, :]
            region[...] = jnp.zeros(region.shape, region.dtype)

    peers = 1
    for a in range(3):
        below = (index[a] + count[a] - 1) // count[a]
        above = (2 * count[a] - 2 - index[a]) // count[a]
        peers = peers * (1 + below + above)
    pl.semaphore_wait(barrier, peers - 1)

    copies = []
    for k, d in enumerate(DIRS):
        sx, sy, sz = (source(a, d[a]) for a in range(3))
        tx, ty, tz = (side(a, -d[a]) for a in range(3))
        copy = pltpu.make_async_remote_copy(
            src_ref=f_ref.at[sz, sy, sx, :],
            dst_ref=p_ref.at[tz, ty, tx, :],
            send_sem=send_sem.at[k],
            recv_sem=recv_sem.at[k],
            device_id=device(d),
            device_id_type=MESH,
        )
        copies.append((d, copy))

        @pl.when(exists(d))
        def _():
            copy.start()

    local.wait()
    for d, copy in copies:
        @pl.when(exists(d))
        def _():
            copy.wait_send()

        @pl.when(exists(tuple(-v for v in d)))
        def _():
            copy.wait_recv()


def with_rim(field, width, collective_id):
    size_z, size_y, size_x, chans = field.shape
    return pl.pallas_call(
        functools.partial(rim_kernel, width),
        out_shape=jax.ShapeDtypeStruct(
            (size_z + 2 * width, size_y + 2 * width, size_x + 2 * width, chans), field.dtype),
        in_specs=[pl.BlockSpec(memory_space=pltpu.VMEM)],
        out_specs=pl.BlockSpec(memory_space=pltpu.VMEM),
        scratch_shapes=[
            pltpu.SemaphoreType.DMA((1,)),
            pltpu.SemaphoreType.DMA((len(DIRS),)),
            pltpu.SemaphoreType.DMA((len(DIRS),)),
        ],
        compiler_params=pltpu.CompilerParams(collective_id=collective_id, has_side_effects=True),
    )(field)


def region_mask(tissue, repeats, block_starts, extents, margin):
    padded = jnp.pad(tissue, 1)
    counts = [extents[d] // repeats[d] + 2 for d in range(3)]
    starts = [jnp.asarray(block_starts[d], dtype=jnp.int32) for d in range(3)]
    table = lax.dynamic_slice(padded, starts, counts)
    for d in range(3):
        table = jnp.repeat(table, repeats[d], axis=d)
    table = table[
        repeats[0] - margin : repeats[0] + extents[0] + margin,
        repeats[1] - margin : repeats[1] + extents[1] + margin,
        repeats[2] - margin : repeats[2] + extents[2] + margin,
    ]
    return table.astype(jnp.float32).transpose(2, 1, 0)[..., None]


def finish(summed, offsets, tissue_mask):
    return (jnp.maximum(summed + offsets, 0.0) * tissue_mask).astype(jnp.bfloat16)


def conv_taps(padded, weights):
    size_z = padded.shape[0] - 2
    stacked = jnp.concatenate([padded[k:k + size_z] for k in range(3)], axis=-1)
    kernel = weights.reshape(3, 3, 3, weights.shape[1], weights.shape[2]).transpose(1, 0, 2, 4, 3)
    kernel = kernel.reshape(3, 3, 3 * weights.shape[2], weights.shape[1])
    return lax.conv_general_dilated(
        stacked, kernel, (1, 1), "VALID",
        dimension_numbers=("NHWC", "HWIO", "NHWC"), preferred_element_type=jnp.float32)


def down_first(grid, weights):
    channels, size_z, size_y, size_x = grid.shape
    split = grid.reshape(channels, size_z // 2, 2, size_y // 2, 2, size_x // 2, 2)
    grouped = weights.reshape(2, 2, 2, weights.shape[1], weights.shape[2])
    return jnp.einsum("abkoi,izkybxa->zyxo", grouped, split, preferred_element_type=jnp.float32)


def down_cells(field, weights):
    size_z, size_y, size_x, channels = field.shape
    split = field.reshape(size_z // 2, 2, size_y // 2, 2, size_x // 2, 2, channels)
    grouped = weights.reshape(2, 2, 2, weights.shape[1], weights.shape[2])
    return jnp.einsum("abkoi,zkybxai->zyxo", grouped, split, preferred_element_type=jnp.float32)


def packed(field):
    size_z, size_y, size_x, chans = field.shape
    return field.transpose(3, 0, 1, 2).reshape(chans, size_z, size_y * size_x)


def local(volume, tissue, w_down1, b_down1, w_conv1a, b_conv1a, w_conv1b, b_conv1b,
          w_down2, b_down2, w_conv2a, b_conv2a, w_conv2b, b_conv2b):
    index_x = lax.axis_index("gx")
    index_y = lax.axis_index("gy")
    index_z = lax.axis_index("gz")
    grid_zero = volume.reshape(volume.shape[0], volume.shape[1], CY, CX)
    first_x = CX // 2
    first_y = CY // 2
    first_z = volume.shape[1] // 2
    first_blocks = (index_x * (first_x // 4), index_y * (first_y // 4), index_z * (first_z // 8))
    mask_one = region_mask(tissue, (4, 4, 8), first_blocks, (first_x, first_y, first_z), 0)
    mask_one_wide = region_mask(tissue, (4, 4, 8), first_blocks, (first_x, first_y, first_z), 1)
    down_one = finish(down_first(grid_zero, w_down1), b_down1, mask_one)
    inner_one = finish(conv_taps(with_rim(down_one, 2, 0), w_conv1a), b_conv1a, mask_one_wide)
    feat_one = finish(conv_taps(inner_one, w_conv1b), b_conv1b, mask_one)
    second_x = first_x // 2
    second_y = first_y // 2
    second_z = first_z // 2
    second_blocks = (index_x * (second_x // 2), index_y * (second_y // 2), index_z * (second_z // 4))
    mask_two = region_mask(tissue, (2, 2, 4), second_blocks, (second_x, second_y, second_z), 0)
    mask_two_wide = region_mask(tissue, (2, 2, 4), second_blocks, (second_x, second_y, second_z), 1)
    down_two = finish(down_cells(feat_one, w_down2), b_down2, mask_two)
    middle = finish(conv_taps(with_rim(down_two, 2, 1), w_conv2a), b_conv2a, mask_two_wide)
    feat_two = finish(conv_taps(middle, w_conv2b), b_conv2b, mask_two)
    return (packed(feat_one), packed(feat_two))


def solution(mesh):
    return jax.shard_map(
        local,
        mesh=mesh,
        in_specs=(P(None, "gz", ("gx", "gy")),) + (P(),) * 13,
        out_specs=(P(None, "gz", ("gx", "gy")), P(None, "gz", ("gx", "gy"))),
        check_vma=False,
    )
```

```python
import functools

import jax
import jax.numpy as jnp
from jax import lax
from jax.experimental import pallas as pl
from jax.experimental.pallas import tpu as pltpu
from jax.sharding import PartitionSpec as P

CX = 64
CY = 32
AXES = ("gx", "gy", "gz")
MESH = pl.DeviceIdType.MESH
DIRS = [
    (dx, dy, dz)
    for dx in (-1, 0, 1)
    for dy in (-1, 0, 1)
    for dz in (-1, 0, 1)
    if (dx, dy, dz) != (0, 0, 0)
]


def rim_kernel(width, f_ref, p_ref, send_sem, recv_sem):
    size_z, size_y, size_x, _ = f_ref.shape
    sizes = (size_x, size_y, size_z)
    index = [lax.axis_index(a) for a in AXES]
    count = [lax.axis_size(a) for a in AXES]

    def exists(d):
        ok = True
        for a in range(3):
            if d[a] == -1:
                ok = jnp.logical_and(ok, index[a] > 0)
            elif d[a] == 1:
                ok = jnp.logical_and(ok, index[a] < count[a] - 1)
        return ok

    def device(d):
        return tuple(index[a] + d[a] for a in range(3))

    def source(a, step):
        s = sizes[a]
        if step == -1:
            return slice(0, width)
        if step == 1:
            return slice(s - width, s)
        return slice(0, s)

    def side(a, step):
        s = sizes[a]
        if step == -1:
            return slice(0, width)
        if step == 1:
            return slice(s + width, s + 2 * width)
        return slice(width, width + s)

    barrier = pltpu.get_barrier_semaphore()
    for d in DIRS:
        @pl.when(exists(d))
        def _():
            pl.semaphore_signal(barrier, inc=1, device_id=device(d), device_id_type=MESH)

    p_ref[width:width + size_z, width:width + size_y, width:width + size_x, :] = f_ref[...]

    for d in DIRS:
        @pl.when(jnp.logical_not(exists(d)))
        def _():
            sx, sy, sz = (side(a, d[a]) for a in range(3))
            region = p_ref.at[sz, sy, sx, :]
            region[...] = jnp.zeros(region.shape, region.dtype)

    peers = 1
    for a in range(3):
        below = (index[a] + count[a] - 1) // count[a]
        above = (2 * count[a] - 2 - index[a]) // count[a]
        peers = peers * (1 + below + above)
    pl.semaphore_wait(barrier, peers - 1)

    copies = []
    for k, d in enumerate(DIRS):
        sx, sy, sz = (source(a, d[a]) for a in range(3))
        tx, ty, tz = (side(a, -d[a]) for a in range(3))
        copy = pltpu.make_async_remote_copy(
            src_ref=f_ref.at[sz, sy, sx, :],
            dst_ref=p_ref.at[tz, ty, tx, :],
            send_sem=send_sem.at[k],
            recv_sem=recv_sem.at[k],
            device_id=device(d),
            device_id_type=MESH,
        )
        copies.append((d, copy))

        @pl.when(exists(d))
        def _():
            copy.start()

    for d, copy in copies:
        @pl.when(exists(d))
        def _():
            copy.wait_send()

        @pl.when(exists(tuple(-v for v in d)))
        def _():
            copy.wait_recv()


def with_rim(field, width, collective_id):
    size_z, size_y, size_x, chans = field.shape
    return pl.pallas_call(
        functools.partial(rim_kernel, width),
        out_shape=jax.ShapeDtypeStruct(
            (size_z + 2 * width, size_y + 2 * width, size_x + 2 * width, chans), field.dtype),
        in_specs=[pl.BlockSpec(memory_space=pltpu.VMEM)],
        out_specs=pl.BlockSpec(memory_space=pltpu.VMEM),
        scratch_shapes=[
            pltpu.SemaphoreType.DMA((len(DIRS),)),
            pltpu.SemaphoreType.DMA((len(DIRS),)),
        ],
        compiler_params=pltpu.CompilerParams(collective_id=collective_id, has_side_effects=True),
    )(field)


def region_mask(tissue, repeats, block_starts, extents, margin):
    padded = jnp.pad(tissue, 1)
    counts = [extents[d] // repeats[d] + 2 for d in range(3)]
    starts = [jnp.asarray(block_starts[d], dtype=jnp.int32) for d in range(3)]
    table = lax.dynamic_slice(padded, starts, counts)
    for d in range(3):
        table = jnp.repeat(table, repeats[d], axis=d)
    table = table[
        repeats[0] - margin : repeats[0] + extents[0] + margin,
        repeats[1] - margin : repeats[1] + extents[1] + margin,
        repeats[2] - margin : repeats[2] + extents[2] + margin,
    ]
    return table.astype(jnp.float32).transpose(2, 1, 0)[..., None]


def finish(summed, offsets, tissue_mask):
    return (jnp.maximum(summed + offsets, 0.0) * tissue_mask).astype(jnp.bfloat16)


def conv_taps(padded, weights):
    size_z = padded.shape[0] - 2
    stacked = jnp.concatenate([padded[k:k + size_z] for k in range(3)], axis=-1)
    kernel = weights.reshape(3, 3, 3, weights.shape[1], weights.shape[2]).transpose(1, 0, 2, 4, 3)
    kernel = kernel.reshape(3, 3, 3 * weights.shape[2], weights.shape[1])
    return lax.conv_general_dilated(
        stacked, kernel, (1, 1), "VALID",
        dimension_numbers=("NHWC", "HWIO", "NHWC"), preferred_element_type=jnp.float32)


def down_first(grid, weights):
    channels, size_z, size_y, size_x = grid.shape
    split = grid.reshape(channels, size_z // 2, 2, size_y // 2, 2, size_x // 2, 2)
    grouped = weights.reshape(2, 2, 2, weights.shape[1], weights.shape[2])
    return jnp.einsum("abkoi,izkybxa->zyxo", grouped, split, preferred_element_type=jnp.float32)


def down_cells(field, weights):
    size_z, size_y, size_x, channels = field.shape
    split = field.reshape(size_z // 2, 2, size_y // 2, 2, size_x // 2, 2, channels)
    grouped = weights.reshape(2, 2, 2, weights.shape[1], weights.shape[2])
    return jnp.einsum("abkoi,zkybxai->zyxo", grouped, split, preferred_element_type=jnp.float32)


def packed(field):
    size_z, size_y, size_x, chans = field.shape
    return field.transpose(3, 0, 1, 2).reshape(chans, size_z, size_y * size_x)


def local(volume, tissue, w_down1, b_down1, w_conv1a, b_conv1a, w_conv1b, b_conv1b,
          w_down2, b_down2, w_conv2a, b_conv2a, w_conv2b, b_conv2b):
    index_x = lax.axis_index("gx")
    index_y = lax.axis_index("gy")
    index_z = lax.axis_index("gz")
    grid_zero = volume.reshape(volume.shape[0], volume.shape[1], CY, CX)
    first_x = CX // 2
    first_y = CY // 2
    first_z = volume.shape[1] // 2
    first_blocks = (index_x * (first_x // 4), index_y * (first_y // 4), index_z * (first_z // 8))
    mask_one = region_mask(tissue, (4, 4, 8), first_blocks, (first_x, first_y, first_z), 0)
    mask_one_wide = region_mask(tissue, (4, 4, 8), first_blocks, (first_x, first_y, first_z), 1)
    down_one = finish(down_first(grid_zero, w_down1), b_down1, mask_one)
    inner_one = finish(conv_taps(with_rim(down_one, 2, 0), w_conv1a), b_conv1a, mask_one_wide)
    feat_one = finish(conv_taps(inner_one, w_conv1b), b_conv1b, mask_one)
    second_x = first_x // 2
    second_y = first_y // 2
    second_z = first_z // 2
    second_blocks = (index_x * (second_x // 2), index_y * (second_y // 2), index_z * (second_z // 4))
    mask_two = region_mask(tissue, (2, 2, 4), second_blocks, (second_x, second_y, second_z), 0)
    mask_two_wide = region_mask(tissue, (2, 2, 4), second_blocks, (second_x, second_y, second_z), 1)
    down_two = finish(down_cells(feat_one, w_down2), b_down2, mask_two)
    middle = finish(conv_taps(with_rim(down_two, 2, 1), w_conv2a), b_conv2a, mask_two_wide)
    feat_two = finish(conv_taps(middle, w_conv2b), b_conv2b, mask_two)
    return (packed(feat_one), packed(feat_two))


def solution(mesh):
    return jax.shard_map(
        local,
        mesh=mesh,
        in_specs=(P(None, "gz", ("gx", "gy")),) + (P(),) * 13,
        out_specs=(P(None, "gz", ("gx", "gy")), P(None, "gz", ("gx", "gy"))),
        check_vma=False,
    )
```

```python
import functools

import jax
import jax.numpy as jnp
from jax import lax
from jax.experimental import pallas as pl
from jax.experimental.pallas import tpu as pltpu
from jax.sharding import PartitionSpec as P

CX = 64
CY = 32
AXES = ("gx", "gy", "gz")
MESH = pl.DeviceIdType.MESH
DIRS = [
    (dx, dy, dz)
    for dx in (-1, 0, 1)
    for dy in (-1, 0, 1)
    for dz in (-1, 0, 1)
    if (dx, dy, dz) != (0, 0, 0)
]


def rim_kernel(width, f_ref, p_ref, send_sem, recv_sem):
    size_z, size_y, size_x, _ = f_ref.shape
    sizes = (size_x, size_y, size_z)
    index = [lax.axis_index(a) for a in AXES]
    count = [lax.axis_size(a) for a in AXES]

    def exists(d):
        ok = True
        for a in range(3):
            if d[a] == -1:
                ok = jnp.logical_and(ok, index[a] > 0)
            elif d[a] == 1:
                ok = jnp.logical_and(ok, index[a] < count[a] - 1)
        return ok

    def device(d):
        return tuple(index[a] + d[a] for a in range(3))

    def source(a, step):
        s = sizes[a]
        if step == -1:
            return slice(0, width)
        if step == 1:
            return slice(s - width, s)
        return slice(0, s)

    def side(a, step):
        s = sizes[a]
        if step == -1:
            return slice(0, width)
        if step == 1:
            return slice(s + width, s + 2 * width)
        return slice(width, width + s)

    barrier = pltpu.get_barrier_semaphore()
    for d in DIRS:
        @pl.when(exists(d))
        def _():
            pl.semaphore_signal(barrier, inc=1, device_id=device(d), device_id_type=MESH)

    p_ref[width:width + size_z, width:width + size_y, width:width + size_x, :] = f_ref[...]

    for d in DIRS:
        @pl.when(jnp.logical_not(exists(d)))
        def _():
            sx, sy, sz = (side(a, d[a]) for a in range(3))
            region = p_ref.at[sz, sy, sx, :]
            region[...] = jnp.zeros(region.shape, region.dtype)

    peers = 1
    for a in range(3):
        below = (index[a] + count[a] - 1) // count[a]
        above = (2 * count[a] - 2 - index[a]) // count[a]
        peers = peers * (1 + below + above)
    pl.semaphore_wait(barrier, peers - 1)

    copies = []
    for k, d in enumerate(DIRS):
        sx, sy, sz = (source(a, d[a]) for a in range(3))
        tx, ty, tz = (side(a, -d[a]) for a in range(3))
        copy = pltpu.make_async_remote_copy(
            src_ref=f_ref.at[sz, sy, sx, :],
            dst_ref=p_ref.at[tz, ty, tx, :],
            send_sem=send_sem.at[k],
            recv_sem=recv_sem.at[k],
            device_id=device(d),
            device_id_type=MESH,
        )
        copies.append((d, copy))

        @pl.when(exists(d))
        def _():
            copy.start()

    for d, copy in copies:
        @pl.when(exists(d))
        def _():
            copy.wait_send()

        @pl.when(exists(tuple(-v for v in d)))
        def _():
            copy.wait_recv()


def with_rim(field, width, collective_id):
    size_z, size_y, size_x, chans = field.shape
    return pl.pallas_call(
        functools.partial(rim_kernel, width),
        out_shape=jax.ShapeDtypeStruct(
            (size_z + 2 * width, size_y + 2 * width, size_x + 2 * width, chans), field.dtype),
        in_specs=[pl.BlockSpec(memory_space=pltpu.VMEM)],
        out_specs=pl.BlockSpec(memory_space=pltpu.VMEM),
        scratch_shapes=[
            pltpu.SemaphoreType.DMA((len(DIRS),)),
            pltpu.SemaphoreType.DMA((len(DIRS),)),
        ],
        compiler_params=pltpu.CompilerParams(collective_id=collective_id, has_side_effects=True),
    )(field)


def region_mask(tissue, repeats, block_starts, extents, margin):
    padded = jnp.pad(tissue, 1)
    counts = [extents[d] // repeats[d] + 2 for d in range(3)]
    starts = [jnp.asarray(block_starts[d], dtype=jnp.int32) for d in range(3)]
    table = lax.dynamic_slice(padded, starts, counts)
    for d in range(3):
        table = jnp.repeat(table, repeats[d], axis=d)
    table = table[
        repeats[0] - margin : repeats[0] + extents[0] + margin,
        repeats[1] - margin : repeats[1] + extents[1] + margin,
        repeats[2] - margin : repeats[2] + extents[2] + margin,
    ]
    return table.astype(jnp.float32).transpose(2, 1, 0)[..., None]


def finish(summed, offsets, tissue_mask):
    return (jnp.maximum(summed + offsets, 0.0) * tissue_mask).astype(jnp.bfloat16)


def conv_taps(padded, weights):
    size_z = padded.shape[0] - 2
    kernel = weights.reshape(3, 3, 3, weights.shape[1], weights.shape[2]).transpose(2, 1, 0, 4, 3)
    total = None
    for k in range(3):
        term = lax.conv_general_dilated(
            padded[k:k + size_z], kernel[k], (1, 1), "VALID",
            dimension_numbers=("NHWC", "HWIO", "NHWC"), preferred_element_type=jnp.float32)
        total = term if total is None else total + term
    return total


def down_first(grid, weights):
    channels, size_z, size_y, size_x = grid.shape
    split = grid.reshape(channels, size_z // 2, 2, size_y // 2, 2, size_x // 2, 2)
    grouped = weights.reshape(2, 2, 2, weights.shape[1], weights.shape[2])
    return jnp.einsum("abkoi,izkybxa->zyxo", grouped, split, preferred_element_type=jnp.float32)


def down_cells(field, weights):
    size_z, size_y, size_x, channels = field.shape
    split = field.reshape(size_z // 2, 2, size_y // 2, 2, size_x // 2, 2, channels)
    grouped = weights.reshape(2, 2, 2, weights.shape[1], weights.shape[2])
    return jnp.einsum("abkoi,zkybxai->zyxo", grouped, split, preferred_element_type=jnp.float32)


def packed(field):
    size_z, size_y, size_x, chans = field.shape
    return field.transpose(3, 0, 1, 2).reshape(chans, size_z, size_y * size_x)


def local(volume, tissue, w_down1, b_down1, w_conv1a, b_conv1a, w_conv1b, b_conv1b,
          w_down2, b_down2, w_conv2a, b_conv2a, w_conv2b, b_conv2b):
    index_x = lax.axis_index("gx")
    index_y = lax.axis_index("gy")
    index_z = lax.axis_index("gz")
    grid_zero = volume.reshape(volume.shape[0], volume.shape[1], CY, CX)
    first_x = CX // 2
    first_y = CY // 2
    first_z = volume.shape[1] // 2
    first_blocks = (index_x * (first_x // 4), index_y * (first_y // 4), index_z * (first_z // 8))
    mask_one = region_mask(tissue, (4, 4, 8), first_blocks, (first_x, first_y, first_z), 0)
    mask_one_wide = region_mask(tissue, (4, 4, 8), first_blocks, (first_x, first_y, first_z), 1)
    down_one = finish(down_first(grid_zero, w_down1), b_down1, mask_one)
    inner_one = finish(conv_taps(with_rim(down_one, 2, 0), w_conv1a), b_conv1a, mask_one_wide)
    feat_one = finish(conv_taps(inner_one, w_conv1b), b_conv1b, mask_one)
    second_x = first_x // 2
    second_y = first_y // 2
    second_z = first_z // 2
    second_blocks = (index_x * (second_x // 2), index_y * (second_y // 2), index_z * (second_z // 4))
    mask_two = region_mask(tissue, (2, 2, 4), second_blocks, (second_x, second_y, second_z), 0)
    mask_two_wide = region_mask(tissue, (2, 2, 4), second_blocks, (second_x, second_y, second_z), 1)
    down_two = finish(down_cells(feat_one, w_down2), b_down2, mask_two)
    middle = finish(conv_taps(with_rim(down_two, 2, 1), w_conv2a), b_conv2a, mask_two_wide)
    feat_two = finish(conv_taps(middle, w_conv2b), b_conv2b, mask_two)
    return (packed(feat_one), packed(feat_two))


def solution(mesh):
    return jax.shard_map(
        local,
        mesh=mesh,
        in_specs=(P(None, "gz", ("gx", "gy")),) + (P(),) * 13,
        out_specs=(P(None, "gz", ("gx", "gy")), P(None, "gz", ("gx", "gy"))),
        check_vma=False,
    )
```

```python
import functools

import jax
import jax.numpy as jnp
from jax import lax
from jax.experimental import pallas as pl
from jax.experimental.pallas import tpu as pltpu
from jax.sharding import PartitionSpec as P

CX = 64
CY = 32
AXES = ("gx", "gy", "gz")
MESH = pl.DeviceIdType.MESH
DIRS = [
    (dx, dy, dz)
    for dx in (-1, 0, 1)
    for dy in (-1, 0, 1)
    for dz in (-1, 0, 1)
    if (dx, dy, dz) != (0, 0, 0)
]


def rim_kernel(width, owners, f_ref, p_ref, local_sem, send_sem, recv_sem):
    sizes = f_ref.shape[:3]
    index = [lax.axis_index(a) for a in AXES]
    count = [lax.axis_size(a) for a in AXES]

    def exists(d):
        ok = True
        for a in range(3):
            if d[a] == -1:
                ok = jnp.logical_and(ok, index[a] > 0)
            elif d[a] == 1:
                ok = jnp.logical_and(ok, index[a] < count[a] - 1)
        return ok

    def device(d):
        return tuple(index[a] + d[a] for a in range(3))

    def source(k, step):
        s = sizes[k]
        if step == -1:
            return slice(0, width)
        if step == 1:
            return slice(s - width, s)
        return slice(0, s)

    def side(k, step):
        s = sizes[k]
        if step == -1:
            return slice(0, width)
        if step == 1:
            return slice(s + width, s + 2 * width)
        return slice(width, width + s)

    def window(pick, d, sign):
        return tuple(pick(k, sign * d[owners[k]]) for k in range(3)) + (slice(None),)

    barrier = pltpu.get_barrier_semaphore()
    for d in DIRS:
        @pl.when(exists(d))
        def _():
            pl.semaphore_signal(barrier, inc=1, device_id=device(d), device_id_type=MESH)

    interior = tuple(slice(width, width + sizes[k]) for k in range(3)) + (slice(None),)
    local = pltpu.make_async_copy(f_ref, p_ref.at[interior], local_sem.at[0])
    local.start()

    for d in DIRS:
        @pl.when(jnp.logical_not(exists(d)))
        def _():
            region = p_ref.at[window(side, d, 1)]
            region[...] = jnp.zeros(region.shape, region.dtype)

    peers = 1
    for a in range(3):
        below = (index[a] + count[a] - 1) // count[a]
        above = (2 * count[a] - 2 - index[a]) // count[a]
        peers = peers * (1 + below + above)
    pl.semaphore_wait(barrier, peers - 1)

    copies = []
    for k, d in enumerate(DIRS):
        copy = pltpu.make_async_remote_copy(
            src_ref=f_ref.at[window(source, d, 1)],
            dst_ref=p_ref.at[window(side, d, -1)],
            send_sem=send_sem.at[k],
            recv_sem=recv_sem.at[k],
            device_id=device(d),
            device_id_type=MESH,
        )
        copies.append((d, copy))

        @pl.when(exists(d))
        def _():
            copy.start()

    local.wait()
    for d, copy in copies:
        @pl.when(exists(d))
        def _():
            copy.wait_send()

        @pl.when(exists(tuple(-v for v in d)))
        def _():
            copy.wait_recv()


def with_rim(field, width, owners, collective_id):
    sizes = field.shape[:3]
    return pl.pallas_call(
        functools.partial(rim_kernel, width, owners),
        out_shape=jax.ShapeDtypeStruct(
            tuple(s + 2 * width for s in sizes) + (field.shape[3],), field.dtype),
        in_specs=[pl.BlockSpec(memory_space=pltpu.VMEM)],
        out_specs=pl.BlockSpec(memory_space=pltpu.VMEM),
        scratch_shapes=[
            pltpu.SemaphoreType.DMA((1,)),
            pltpu.SemaphoreType.DMA((len(DIRS),)),
            pltpu.SemaphoreType.DMA((len(DIRS),)),
        ],
        compiler_params=pltpu.CompilerParams(collective_id=collective_id, has_side_effects=True),
    )(field)


def rim_yxz(field, width, collective_id):
    rimmed = with_rim(field.transpose(1, 2, 0, 3), width, (1, 0, 2), collective_id)
    return rimmed.transpose(2, 0, 1, 3)


def region_mask(tissue, repeats, block_starts, extents, margin):
    padded = jnp.pad(tissue, 1)
    counts = [extents[d] // repeats[d] + 2 for d in range(3)]
    starts = [jnp.asarray(block_starts[d], dtype=jnp.int32) for d in range(3)]
    table = lax.dynamic_slice(padded, starts, counts)
    for d in range(3):
        table = jnp.repeat(table, repeats[d], axis=d)
    table = table[
        repeats[0] - margin : repeats[0] + extents[0] + margin,
        repeats[1] - margin : repeats[1] + extents[1] + margin,
        repeats[2] - margin : repeats[2] + extents[2] + margin,
    ]
    return table.astype(jnp.float32).transpose(2, 1, 0)[..., None]


def finish(summed, offsets, tissue_mask):
    return (jnp.maximum(summed + offsets, 0.0) * tissue_mask).astype(jnp.bfloat16)


def conv_taps(padded, weights):
    size_z = padded.shape[0] - 2
    stacked = jnp.concatenate([padded[k:k + size_z] for k in range(3)], axis=-1)
    kernel = weights.reshape(3, 3, 3, weights.shape[1], weights.shape[2]).transpose(1, 0, 2, 4, 3)
    kernel = kernel.reshape(3, 3, 3 * weights.shape[2], weights.shape[1])
    return lax.conv_general_dilated(
        stacked, kernel, (1, 1), "VALID",
        dimension_numbers=("NHWC", "HWIO", "NHWC"), preferred_element_type=jnp.float32)


def down_first(grid, weights):
    channels, size_z, size_y, size_x = grid.shape
    split = grid.reshape(channels, size_z // 2, 2, size_y // 2, 2, size_x // 2, 2)
    grouped = weights.reshape(2, 2, 2, weights.shape[1], weights.shape[2])
    return jnp.einsum("abkoi,izkybxa->zyxo", grouped, split, preferred_element_type=jnp.float32)


def down_cells(field, weights):
    size_z, size_y, size_x, channels = field.shape
    split = field.reshape(size_z // 2, 2, size_y // 2, 2, size_x // 2, 2, channels)
    grouped = weights.reshape(2, 2, 2, weights.shape[1], weights.shape[2])
    return jnp.einsum("abkoi,zkybxai->zyxo", grouped, split, preferred_element_type=jnp.float32)


def packed(field):
    size_z, size_y, size_x, chans = field.shape
    return field.transpose(3, 0, 1, 2).reshape(chans, size_z, size_y * size_x)


def local(volume, tissue, w_down1, b_down1, w_conv1a, b_conv1a, w_conv1b, b_conv1b,
          w_down2, b_down2, w_conv2a, b_conv2a, w_conv2b, b_conv2b):
    index_x = lax.axis_index("gx")
    index_y = lax.axis_index("gy")
    index_z = lax.axis_index("gz")
    grid_zero = volume.reshape(volume.shape[0], volume.shape[1], CY, CX)
    first_x = CX // 2
    first_y = CY // 2
    first_z = volume.shape[1] // 2
    first_blocks = (index_x * (first_x // 4), index_y * (first_y // 4), index_z * (first_z // 8))
    mask_one = region_mask(tissue, (4, 4, 8), first_blocks, (first_x, first_y, first_z), 0)
    mask_one_wide = region_mask(tissue, (4, 4, 8), first_blocks, (first_x, first_y, first_z), 1)
    down_one = finish(down_first(grid_zero, w_down1), b_down1, mask_one)
    inner_one = finish(conv_taps(rim_yxz(down_one, 2, 0), w_conv1a), b_conv1a, mask_one_wide)
    feat_one = finish(conv_taps(inner_one, w_conv1b), b_conv1b, mask_one)
    second_x = first_x // 2
    second_y = first_y // 2
    second_z = first_z // 2
    second_blocks = (index_x * (second_x // 2), index_y * (second_y // 2), index_z * (second_z // 4))
    mask_two = region_mask(tissue, (2, 2, 4), second_blocks, (second_x, second_y, second_z), 0)
    mask_two_wide = region_mask(tissue, (2, 2, 4), second_blocks, (second_x, second_y, second_z), 1)
    down_two = finish(down_cells(feat_one, w_down2), b_down2, mask_two)
    middle = finish(conv_taps(with_rim(down_two, 2, (2, 1, 0), 1), w_conv2a), b_conv2a, mask_two_wide)
    feat_two = finish(conv_taps(middle, w_conv2b), b_conv2b, mask_two)
    return (packed(feat_one), packed(feat_two))


def solution(mesh):
    return jax.shard_map(
        local,
        mesh=mesh,
        in_specs=(P(None, "gz", ("gx", "gy")),) + (P(),) * 13,
        out_specs=(P(None, "gz", ("gx", "gy")), P(None, "gz", ("gx", "gy"))),
        check_vma=False,
    )
```

```python
import functools

import jax
import jax.numpy as jnp
from jax import lax
from jax.experimental import pallas as pl
from jax.experimental.pallas import tpu as pltpu
from jax.sharding import PartitionSpec as P

CX = 64
CY = 32
AXES = ("gx", "gy", "gz")
MESH = pl.DeviceIdType.MESH
DIRS = [
    (dx, dy, dz)
    for dx in (-1, 0, 1)
    for dy in (-1, 0, 1)
    for dz in (-1, 0, 1)
    if (dx, dy, dz) != (0, 0, 0)
]


def rim_kernel(width, f_ref, p_ref, local_sem, send_sem, recv_sem):
    size_z, size_y, size_x, _ = f_ref.shape
    sizes = (size_x, size_y, size_z)
    index = [lax.axis_index(a) for a in AXES]
    count = [lax.axis_size(a) for a in AXES]

    def exists(d):
        ok = True
        for a in range(3):
            if d[a] == -1:
                ok = jnp.logical_and(ok, index[a] > 0)
            elif d[a] == 1:
                ok = jnp.logical_and(ok, index[a] < count[a] - 1)
        return ok

    def device(d):
        return tuple(index[a] + d[a] for a in range(3))

    def source(a, step):
        s = sizes[a]
        if step == -1:
            return slice(0, width)
        if step == 1:
            return slice(s - width, s)
        return slice(0, s)

    def side(a, step):
        s = sizes[a]
        if step == -1:
            return slice(0, width)
        if step == 1:
            return slice(s + width, s + 2 * width)
        return slice(width, width + s)

    barrier = pltpu.get_barrier_semaphore()
    for d in DIRS:
        @pl.when(exists(d))
        def _():
            pl.semaphore_signal(barrier, inc=1, device_id=device(d), device_id_type=MESH)

    local = pltpu.make_async_copy(
        f_ref, p_ref.at[width:width + size_z, width:width + size_y, width:width + size_x, :],
        local_sem.at[0])
    local.start()

    for d in DIRS:
        @pl.when(jnp.logical_not(exists(d)))
        def _():
            sx, sy, sz = (side(a, d[a]) for a in range(3))
            region = p_ref.at[sz, sy, sx, :]
            region[...] = jnp.zeros(region.shape, region.dtype)

    peers = 1
    for a in range(3):
        below = (index[a] + count[a] - 1) // count[a]
        above = (2 * count[a] - 2 - index[a]) // count[a]
        peers = peers * (1 + below + above)
    pl.semaphore_wait(barrier, peers - 1)

    copies = []
    for k, d in enumerate(DIRS):
        sx, sy, sz = (source(a, d[a]) for a in range(3))
        tx, ty, tz = (side(a, -d[a]) for a in range(3))
        copy = pltpu.make_async_remote_copy(
            src_ref=f_ref.at[sz, sy, sx, :],
            dst_ref=p_ref.at[tz, ty, tx, :],
            send_sem=send_sem.at[k],
            recv_sem=recv_sem.at[k],
            device_id=device(d),
            device_id_type=MESH,
        )
        copies.append((d, copy))

        @pl.when(exists(d))
        def _():
            copy.start()

    local.wait()
    for d, copy in copies:
        @pl.when(exists(d))
        def _():
            copy.wait_send()

        @pl.when(exists(tuple(-v for v in d)))
        def _():
            copy.wait_recv()


def with_rim(field, width, collective_id):
    size_z, size_y, size_x, chans = field.shape
    return pl.pallas_call(
        functools.partial(rim_kernel, width),
        out_shape=jax.ShapeDtypeStruct(
            (size_z + 2 * width, size_y + 2 * width, size_x + 2 * width, chans), field.dtype),
        in_specs=[pl.BlockSpec(memory_space=pltpu.VMEM)],
        out_specs=pl.BlockSpec(memory_space=pltpu.VMEM),
        scratch_shapes=[
            pltpu.SemaphoreType.DMA((1,)),
            pltpu.SemaphoreType.DMA((len(DIRS),)),
            pltpu.SemaphoreType.DMA((len(DIRS),)),
        ],
        compiler_params=pltpu.CompilerParams(collective_id=collective_id, has_side_effects=True),
    )(field)


def region_mask(tissue, repeats, block_starts, extents, margin):
    padded = jnp.pad(tissue, 1)
    counts = [extents[d] // repeats[d] + 2 for d in range(3)]
    starts = [jnp.asarray(block_starts[d], dtype=jnp.int32) for d in range(3)]
    table = lax.dynamic_slice(padded, starts, counts)
    for d in range(3):
        table = jnp.repeat(table, repeats[d], axis=d)
    table = table[
        repeats[0] - margin : repeats[0] + extents[0] + margin,
        repeats[1] - margin : repeats[1] + extents[1] + margin,
        repeats[2] - margin : repeats[2] + extents[2] + margin,
    ]
    return table.astype(jnp.float32).transpose(2, 1, 0)[..., None]


def finish(summed, offsets, tissue_mask):
    return (jnp.maximum(summed + offsets, 0.0) * tissue_mask).astype(jnp.bfloat16)


def conv_taps(padded, weights):
    size_z = padded.shape[0] - 2
    stacked = jnp.concatenate([padded[k:k + size_z] for k in range(3)], axis=-1)
    kernel = weights.reshape(3, 3, 3, weights.shape[1], weights.shape[2]).transpose(1, 0, 2, 4, 3)
    kernel = kernel.reshape(3, 3, 3 * weights.shape[2], weights.shape[1])
    return lax.conv_general_dilated(
        stacked, kernel, (1, 1), "VALID",
        dimension_numbers=("NHWC", "HWIO", "NHWC"), preferred_element_type=jnp.float32)


def down_kernel(v_ref, w_ref, o_ref, acc_ref):
    half_z, half_y, half_x, outs = o_ref.shape
    size_y, size_x = 2 * half_y, 2 * half_x

    for zp in range(half_z):
        for k in range(2):
            cells = v_ref[:, 2 * zp + k, :]
            for a in range(2):
                for b in range(2):
                    term = lax.dot_general(
                        cells, w_ref[4 * a + 2 * b + k], (((0,), (0,)), ((), ())),
                        preferred_element_type=jnp.float32).reshape(size_y, size_x, outs)
                    if k == 0:
                        acc_ref[2 * a + b] = term
                    else:
                        acc_ref[2 * a + b] += term
        total = None
        for a in range(2):
            for b in range(2):
                part = acc_ref[2 * a + b, pl.ds(b, half_y, stride=2), pl.ds(a, half_x, stride=2), :]
                total = part if total is None else total + part
        o_ref[zp] = total


def down_first(volume, weights):
    chans, size_z, cells = volume.shape
    size_y = cells // CX
    outs = weights.shape[1]
    return pl.pallas_call(
        down_kernel,
        out_shape=jax.ShapeDtypeStruct((size_z // 2, size_y // 2, CX // 2, outs), jnp.float32),
        in_specs=[pl.BlockSpec(memory_space=pltpu.VMEM)] * 2,
        out_specs=pl.BlockSpec(memory_space=pltpu.VMEM),
        scratch_shapes=[pltpu.VMEM((4, size_y, CX, outs), jnp.float32)],
    )(volume, weights.transpose(0, 2, 1))


def down_cells(field, weights):
    size_z, size_y, size_x, channels = field.shape
    split = field.reshape(size_z // 2, 2, size_y // 2, 2, size_x // 2, 2, channels)
    grouped = weights.reshape(2, 2, 2, weights.shape[1], weights.shape[2])
    return jnp.einsum("abkoi,zkybxai->zyxo", grouped, split, preferred_element_type=jnp.float32)


def packed(field):
    size_z, size_y, size_x, chans = field.shape
    return field.transpose(3, 0, 1, 2).reshape(chans, size_z, size_y * size_x)


def local(volume, tissue, w_down1, b_down1, w_conv1a, b_conv1a, w_conv1b, b_conv1b,
          w_down2, b_down2, w_conv2a, b_conv2a, w_conv2b, b_conv2b):
    index_x = lax.axis_index("gx")
    index_y = lax.axis_index("gy")
    index_z = lax.axis_index("gz")
    grid_zero = volume.reshape(volume.shape[0], volume.shape[1], CY, CX)
    first_x = CX // 2
    first_y = CY // 2
    first_z = volume.shape[1] // 2
    first_blocks = (index_x * (first_x // 4), index_y * (first_y // 4), index_z * (first_z // 8))
    mask_one = region_mask(tissue, (4, 4, 8), first_blocks, (first_x, first_y, first_z), 0)
    mask_one_wide = region_mask(tissue, (4, 4, 8), first_blocks, (first_x, first_y, first_z), 1)
    down_one = finish(down_first(volume, w_down1), b_down1, mask_one)
    inner_one = finish(conv_taps(with_rim(down_one, 2, 0), w_conv1a), b_conv1a, mask_one_wide)
    feat_one = finish(conv_taps(inner_one, w_conv1b), b_conv1b, mask_one)
    second_x = first_x // 2
    second_y = first_y // 2
    second_z = first_z // 2
    second_blocks = (index_x * (second_x // 2), index_y * (second_y // 2), index_z * (second_z // 4))
    mask_two = region_mask(tissue, (2, 2, 4), second_blocks, (second_x, second_y, second_z), 0)
    mask_two_wide = region_mask(tissue, (2, 2, 4), second_blocks, (second_x, second_y, second_z), 1)
    down_two = finish(down_cells(feat_one, w_down2), b_down2, mask_two)
    middle = finish(conv_taps(with_rim(down_two, 2, 1), w_conv2a), b_conv2a, mask_two_wide)
    feat_two = finish(conv_taps(middle, w_conv2b), b_conv2b, mask_two)
    return (packed(feat_one), packed(feat_two))


def solution(mesh):
    return jax.shard_map(
        local,
        mesh=mesh,
        in_specs=(P(None, "gz", ("gx", "gy")),) + (P(),) * 13,
        out_specs=(P(None, "gz", ("gx", "gy")), P(None, "gz", ("gx", "gy"))),
        check_vma=False,
    )
```

```python
import functools

import jax
import jax.numpy as jnp
from jax import lax
from jax.experimental import pallas as pl
from jax.experimental.pallas import tpu as pltpu
from jax.sharding import PartitionSpec as P

CX = 64
CY = 32
AXES = ("gx", "gy", "gz")
MESH = pl.DeviceIdType.MESH
DIRS = [
    (dx, dy, dz)
    for dx in (-1, 0, 1)
    for dy in (-1, 0, 1)
    for dz in (-1, 0, 1)
    if (dx, dy, dz) != (0, 0, 0)
]


def rim_kernel(width, f_ref, p_ref, local_sem, send_sem, recv_sem):
    size_z, size_y, size_x, _ = f_ref.shape
    sizes = (size_x, size_y, size_z)
    index = [lax.axis_index(a) for a in AXES]
    count = [lax.axis_size(a) for a in AXES]

    def exists(d):
        ok = True
        for a in range(3):
            if d[a] == -1:
                ok = jnp.logical_and(ok, index[a] > 0)
            elif d[a] == 1:
                ok = jnp.logical_and(ok, index[a] < count[a] - 1)
        return ok

    def device(d):
        return tuple(index[a] + d[a] for a in range(3))

    def source(a, step):
        s = sizes[a]
        if step == -1:
            return slice(0, width)
        if step == 1:
            return slice(s - width, s)
        return slice(0, s)

    def side(a, step):
        s = sizes[a]
        if step == -1:
            return slice(0, width)
        if step == 1:
            return slice(s + width, s + 2 * width)
        return slice(width, width + s)

    barrier = pltpu.get_barrier_semaphore()
    for d in DIRS:
        @pl.when(exists(d))
        def _():
            pl.semaphore_signal(barrier, inc=1, device_id=device(d), device_id_type=MESH)

    local = pltpu.make_async_copy(
        f_ref, p_ref.at[width:width + size_z, width:width + size_y, width:width + size_x, :],
        local_sem.at[0])
    local.start()

    for d in DIRS:
        @pl.when(jnp.logical_not(exists(d)))
        def _():
            sx, sy, sz = (side(a, d[a]) for a in range(3))
            region = p_ref.at[sz, sy, sx, :]
            region[...] = jnp.zeros(region.shape, region.dtype)

    peers = 1
    for a in range(3):
        below = (index[a] + count[a] - 1) // count[a]
        above = (2 * count[a] - 2 - index[a]) // count[a]
        peers = peers * (1 + below + above)
    pl.semaphore_wait(barrier, peers - 1)

    copies = []
    for k, d in enumerate(DIRS):
        sx, sy, sz = (source(a, d[a]) for a in range(3))
        tx, ty, tz = (side(a, -d[a]) for a in range(3))
        copy = pltpu.make_async_remote_copy(
            src_ref=f_ref.at[sz, sy, sx, :],
            dst_ref=p_ref.at[tz, ty, tx, :],
            send_sem=send_sem.at[k],
            recv_sem=recv_sem.at[k],
            device_id=device(d),
            device_id_type=MESH,
        )
        copies.append((d, copy))

        @pl.when(exists(d))
        def _():
            copy.start()

    local.wait()
    for d, copy in copies:
        @pl.when(exists(d))
        def _():
            copy.wait_send()

        @pl.when(exists(tuple(-v for v in d)))
        def _():
            copy.wait_recv()


def with_rim(field, width, collective_id):
    size_z, size_y, size_x, chans = field.shape
    return pl.pallas_call(
        functools.partial(rim_kernel, width),
        out_shape=jax.ShapeDtypeStruct(
            (size_z + 2 * width, size_y + 2 * width, size_x + 2 * width, chans), field.dtype),
        in_specs=[pl.BlockSpec(memory_space=pltpu.VMEM)],
        out_specs=pl.BlockSpec(memory_space=pltpu.VMEM),
        scratch_shapes=[
            pltpu.SemaphoreType.DMA((1,)),
            pltpu.SemaphoreType.DMA((len(DIRS),)),
            pltpu.SemaphoreType.DMA((len(DIRS),)),
        ],
        compiler_params=pltpu.CompilerParams(collective_id=collective_id, has_side_effects=True),
    )(field)


def region_mask(tissue, repeats, block_starts, extents, margin):
    padded = jnp.pad(tissue, 1)
    counts = [extents[d] // repeats[d] + 2 for d in range(3)]
    starts = [jnp.asarray(block_starts[d], dtype=jnp.int32) for d in range(3)]
    table = lax.dynamic_slice(padded, starts, counts)
    for d in range(3):
        table = jnp.repeat(table, repeats[d], axis=d)
    table = table[
        repeats[0] - margin : repeats[0] + extents[0] + margin,
        repeats[1] - margin : repeats[1] + extents[1] + margin,
        repeats[2] - margin : repeats[2] + extents[2] + margin,
    ]
    return table.astype(jnp.float32).transpose(2, 1, 0)[..., None]


def finish(summed, offsets, tissue_mask):
    return (jnp.maximum(summed + offsets, 0.0) * tissue_mask).astype(jnp.bfloat16)


def conv_taps(padded, weights):
    size_z = padded.shape[0] - 2
    stacked = jnp.concatenate([padded[k:k + size_z] for k in range(3)], axis=-1)
    kernel = weights.reshape(3, 3, 3, weights.shape[1], weights.shape[2]).transpose(1, 0, 2, 4, 3)
    kernel = kernel.reshape(3, 3, 3 * weights.shape[2], weights.shape[1])
    return lax.conv_general_dilated(
        stacked, kernel, (1, 1), "VALID",
        dimension_numbers=("NHWC", "HWIO", "NHWC"), preferred_element_type=jnp.float32)


def down_kernel(v_ref, w_ref, b_ref, m_ref, o_ref, acc_ref):
    half_z, half_y, half_x, outs = o_ref.shape
    size_y, size_x = 2 * half_y, 2 * half_x
    for zp in range(half_z):
        for k in range(2):
            term = lax.dot_general(
                v_ref[:, 2 * zp + k, :], w_ref[k], (((0,), (0,)), ((), ())),
                preferred_element_type=jnp.float32).reshape(size_y, size_x, 4 * outs)
            for a in range(2):
                piece = term[:, :, 2 * a * outs:(2 * a + 2) * outs]
                if k == 0:
                    acc_ref[a] = piece
                else:
                    acc_ref[a] += piece
        sums = []
        for b in range(2):
            sums.append(sum(
                acc_ref[a, pl.ds(b, half_y, stride=2), pl.ds(a, half_x, stride=2), :] for a in range(2)))
        total = sums[0] + pltpu.roll(sums[1], outs, 2)
        total = total[:, :, :outs]
        o_ref[zp] = (jnp.maximum(total + b_ref[...], 0.0) * m_ref[zp]).astype(o_ref.dtype)


def down_first(volume, weights, offsets, tissue_mask):
    chans, size_z, cells = volume.shape
    size_y = cells // CX
    outs = weights.shape[1]
    grouped = weights.reshape(2, 2, 2, outs, chans).transpose(2, 4, 0, 1, 3).reshape(2, chans, 4 * outs)
    return pl.pallas_call(
        down_kernel,
        out_shape=jax.ShapeDtypeStruct((size_z // 2, size_y // 2, CX // 2, outs), jnp.bfloat16),
        in_specs=[pl.BlockSpec(memory_space=pltpu.VMEM)] * 4,
        out_specs=pl.BlockSpec(memory_space=pltpu.VMEM),
        scratch_shapes=[pltpu.VMEM((2, size_y, CX, 2 * outs), jnp.float32)],
    )(volume, grouped, offsets.reshape(1, outs), tissue_mask)


def down_cells(field, weights):
    size_z, size_y, size_x, channels = field.shape
    split = field.reshape(size_z // 2, 2, size_y // 2, 2, size_x // 2, 2, channels)
    grouped = weights.reshape(2, 2, 2, weights.shape[1], weights.shape[2])
    return jnp.einsum("abkoi,zkybxai->zyxo", grouped, split, preferred_element_type=jnp.float32)


def packed(field):
    size_z, size_y, size_x, chans = field.shape
    return field.transpose(3, 0, 1, 2).reshape(chans, size_z, size_y * size_x)


def local(volume, tissue, w_down1, b_down1, w_conv1a, b_conv1a, w_conv1b, b_conv1b,
          w_down2, b_down2, w_conv2a, b_conv2a, w_conv2b, b_conv2b):
    index_x = lax.axis_index("gx")
    index_y = lax.axis_index("gy")
    index_z = lax.axis_index("gz")
    grid_zero = volume.reshape(volume.shape[0], volume.shape[1], CY, CX)
    first_x = CX // 2
    first_y = CY // 2
    first_z = volume.shape[1] // 2
    first_blocks = (index_x * (first_x // 4), index_y * (first_y // 4), index_z * (first_z // 8))
    mask_one = region_mask(tissue, (4, 4, 8), first_blocks, (first_x, first_y, first_z), 0)
    mask_one_wide = region_mask(tissue, (4, 4, 8), first_blocks, (first_x, first_y, first_z), 1)
    down_one = down_first(volume, w_down1, b_down1, mask_one)
    inner_one = finish(conv_taps(with_rim(down_one, 2, 0), w_conv1a), b_conv1a, mask_one_wide)
    feat_one = finish(conv_taps(inner_one, w_conv1b), b_conv1b, mask_one)
    second_x = first_x // 2
    second_y = first_y // 2
    second_z = first_z // 2
    second_blocks = (index_x * (second_x // 2), index_y * (second_y // 2), index_z * (second_z // 4))
    mask_two = region_mask(tissue, (2, 2, 4), second_blocks, (second_x, second_y, second_z), 0)
    mask_two_wide = region_mask(tissue, (2, 2, 4), second_blocks, (second_x, second_y, second_z), 1)
    down_two = finish(down_cells(feat_one, w_down2), b_down2, mask_two)
    middle = finish(conv_taps(with_rim(down_two, 2, 1), w_conv2a), b_conv2a, mask_two_wide)
    feat_two = finish(conv_taps(middle, w_conv2b), b_conv2b, mask_two)
    return (packed(feat_one), packed(feat_two))


def solution(mesh):
    return jax.shard_map(
        local,
        mesh=mesh,
        in_specs=(P(None, "gz", ("gx", "gy")),) + (P(),) * 13,
        out_specs=(P(None, "gz", ("gx", "gy")), P(None, "gz", ("gx", "gy"))),
        check_vma=False,
    )
```

```python
import functools

import jax
import jax.numpy as jnp
from jax import lax
from jax.experimental import pallas as pl
from jax.experimental.pallas import tpu as pltpu
from jax.sharding import PartitionSpec as P

CX = 64
CY = 32
AXES = ("gx", "gy", "gz")
MESH = pl.DeviceIdType.MESH
DIRS = [
    (dx, dy, dz)
    for dx in (-1, 0, 1)
    for dy in (-1, 0, 1)
    for dz in (-1, 0, 1)
    if (dx, dy, dz) != (0, 0, 0)
]


def rim_kernel(width, f_ref, p_ref, local_sem, send_sem, recv_sem):
    size_z, size_y, size_x, _ = f_ref.shape
    sizes = (size_x, size_y, size_z)
    index = [lax.axis_index(a) for a in AXES]
    count = [lax.axis_size(a) for a in AXES]

    def exists(d):
        ok = True
        for a in range(3):
            if d[a] == -1:
                ok = jnp.logical_and(ok, index[a] > 0)
            elif d[a] == 1:
                ok = jnp.logical_and(ok, index[a] < count[a] - 1)
        return ok

    def device(d):
        return tuple(index[a] + d[a] for a in range(3))

    def source(a, step):
        s = sizes[a]
        if step == -1:
            return slice(0, width)
        if step == 1:
            return slice(s - width, s)
        return slice(0, s)

    def side(a, step):
        s = sizes[a]
        if step == -1:
            return slice(0, width)
        if step == 1:
            return slice(s + width, s + 2 * width)
        return slice(width, width + s)

    barrier = pltpu.get_barrier_semaphore()
    for d in DIRS:
        @pl.when(exists(d))
        def _():
            pl.semaphore_signal(barrier, inc=1, device_id=device(d), device_id_type=MESH)

    local = pltpu.make_async_copy(
        f_ref, p_ref.at[width:width + size_z, width:width + size_y, width:width + size_x, :],
        local_sem.at[0])
    local.start()

    for d in DIRS:
        @pl.when(jnp.logical_not(exists(d)))
        def _():
            sx, sy, sz = (side(a, d[a]) for a in range(3))
            region = p_ref.at[sz, sy, sx, :]
            region[...] = jnp.zeros(region.shape, region.dtype)

    peers = 1
    for a in range(3):
        below = (index[a] + count[a] - 1) // count[a]
        above = (2 * count[a] - 2 - index[a]) // count[a]
        peers = peers * (1 + below + above)
    pl.semaphore_wait(barrier, peers - 1)

    copies = []
    for k, d in enumerate(DIRS):
        sx, sy, sz = (source(a, d[a]) for a in range(3))
        tx, ty, tz = (side(a, -d[a]) for a in range(3))
        copy = pltpu.make_async_remote_copy(
            src_ref=f_ref.at[sz, sy, sx, :],
            dst_ref=p_ref.at[tz, ty, tx, :],
            send_sem=send_sem.at[k],
            recv_sem=recv_sem.at[k],
            device_id=device(d),
            device_id_type=MESH,
        )
        copies.append((d, copy))

        @pl.when(exists(d))
        def _():
            copy.start()

    local.wait()
    for d, copy in copies:
        @pl.when(exists(d))
        def _():
            copy.wait_send()

        @pl.when(exists(tuple(-v for v in d)))
        def _():
            copy.wait_recv()


def with_rim(field, width, collective_id):
    size_z, size_y, size_x, chans = field.shape
    return pl.pallas_call(
        functools.partial(rim_kernel, width),
        out_shape=jax.ShapeDtypeStruct(
            (size_z + 2 * width, size_y + 2 * width, size_x + 2 * width, chans), field.dtype),
        in_specs=[pl.BlockSpec(memory_space=pltpu.VMEM)],
        out_specs=pl.BlockSpec(memory_space=pltpu.VMEM),
        scratch_shapes=[
            pltpu.SemaphoreType.DMA((1,)),
            pltpu.SemaphoreType.DMA((len(DIRS),)),
            pltpu.SemaphoreType.DMA((len(DIRS),)),
        ],
        compiler_params=pltpu.CompilerParams(collective_id=collective_id, has_side_effects=True),
    )(field)


def region_mask(tissue, repeats, block_starts, extents, margin):
    padded = jnp.pad(tissue, 1)
    counts = [extents[d] // repeats[d] + 2 for d in range(3)]
    starts = [jnp.asarray(block_starts[d], dtype=jnp.int32) for d in range(3)]
    table = lax.dynamic_slice(padded, starts, counts)
    for d in range(3):
        table = jnp.repeat(table, repeats[d], axis=d)
    table = table[
        repeats[0] - margin : repeats[0] + extents[0] + margin,
        repeats[1] - margin : repeats[1] + extents[1] + margin,
        repeats[2] - margin : repeats[2] + extents[2] + margin,
    ]
    return table.astype(jnp.float32).transpose(2, 1, 0)[..., None]


def finish(summed, offsets, tissue_mask):
    return (jnp.maximum(summed + offsets, 0.0) * tissue_mask).astype(jnp.bfloat16)


def conv_taps(padded, weights):
    size_z = padded.shape[0] - 2
    stacked = jnp.concatenate([padded[k:k + size_z] for k in range(3)], axis=-1)
    kernel = weights.reshape(3, 3, 3, weights.shape[1], weights.shape[2]).transpose(1, 0, 2, 4, 3)
    kernel = kernel.reshape(3, 3, 3 * weights.shape[2], weights.shape[1])
    return lax.conv_general_dilated(
        stacked, kernel, (1, 1), "VALID",
        dimension_numbers=("NHWC", "HWIO", "NHWC"), preferred_element_type=jnp.float32)


def conv_cube(padded, weights):
    kernel = weights.reshape(3, 3, 3, weights.shape[1], weights.shape[2]).transpose(2, 1, 0, 4, 3)
    result = lax.conv_general_dilated(
        padded[None], kernel, (1, 1, 1), "VALID",
        dimension_numbers=("NDHWC", "DHWIO", "NDHWC"), preferred_element_type=jnp.float32)
    return result[0]


def down_first(grid, weights):
    channels, size_z, size_y, size_x = grid.shape
    split = grid.reshape(channels, size_z // 2, 2, size_y // 2, 2, size_x // 2, 2)
    grouped = weights.reshape(2, 2, 2, weights.shape[1], weights.shape[2])
    return jnp.einsum("abkoi,izkybxa->zyxo", grouped, split, preferred_element_type=jnp.float32)


def down_cells(field, weights):
    size_z, size_y, size_x, channels = field.shape
    split = field.reshape(size_z // 2, 2, size_y // 2, 2, size_x // 2, 2, channels)
    grouped = weights.reshape(2, 2, 2, weights.shape[1], weights.shape[2])
    return jnp.einsum("abkoi,zkybxai->zyxo", grouped, split, preferred_element_type=jnp.float32)


def packed(field):
    size_z, size_y, size_x, chans = field.shape
    return field.transpose(3, 0, 1, 2).reshape(chans, size_z, size_y * size_x)


def local(volume, tissue, w_down1, b_down1, w_conv1a, b_conv1a, w_conv1b, b_conv1b,
          w_down2, b_down2, w_conv2a, b_conv2a, w_conv2b, b_conv2b):
    index_x = lax.axis_index("gx")
    index_y = lax.axis_index("gy")
    index_z = lax.axis_index("gz")
    grid_zero = volume.reshape(volume.shape[0], volume.shape[1], CY, CX)
    first_x = CX // 2
    first_y = CY // 2
    first_z = volume.shape[1] // 2
    first_blocks = (index_x * (first_x // 4), index_y * (first_y // 4), index_z * (first_z // 8))
    mask_one = region_mask(tissue, (4, 4, 8), first_blocks, (first_x, first_y, first_z), 0)
    mask_one_wide = region_mask(tissue, (4, 4, 8), first_blocks, (first_x, first_y, first_z), 1)
    down_one = finish(down_first(grid_zero, w_down1), b_down1, mask_one)
    inner_one = finish(conv_taps(with_rim(down_one, 2, 0), w_conv1a), b_conv1a, mask_one_wide)
    feat_one = finish(conv_taps(inner_one, w_conv1b), b_conv1b, mask_one)
    second_x = first_x // 2
    second_y = first_y // 2
    second_z = first_z // 2
    second_blocks = (index_x * (second_x // 2), index_y * (second_y // 2), index_z * (second_z // 4))
    mask_two = region_mask(tissue, (2, 2, 4), second_blocks, (second_x, second_y, second_z), 0)
    mask_two_wide = region_mask(tissue, (2, 2, 4), second_blocks, (second_x, second_y, second_z), 1)
    down_two = finish(down_cells(feat_one, w_down2), b_down2, mask_two)
    middle = finish(conv_cube(with_rim(down_two, 2, 1), w_conv2a), b_conv2a, mask_two_wide)
    feat_two = finish(conv_cube(middle, w_conv2b), b_conv2b, mask_two)
    return (packed(feat_one), packed(feat_two))


def solution(mesh):
    return jax.shard_map(
        local,
        mesh=mesh,
        in_specs=(P(None, "gz", ("gx", "gy")),) + (P(),) * 13,
        out_specs=(P(None, "gz", ("gx", "gy")), P(None, "gz", ("gx", "gy"))),
        check_vma=False,
    )
```

```python
import functools

import jax
import jax.numpy as jnp
from jax import lax
from jax.experimental import pallas as pl
from jax.experimental.pallas import tpu as pltpu
from jax.sharding import PartitionSpec as P

CX = 64
CY = 32
AXES = ("gx", "gy", "gz")
MESH = pl.DeviceIdType.MESH
DIRS = [
    (dx, dy, dz)
    for dx in (-1, 0, 1)
    for dy in (-1, 0, 1)
    for dz in (-1, 0, 1)
    if (dx, dy, dz) != (0, 0, 0)
]


def rim_kernel(widths, f_ref, p_ref, local_sem, send_sem, recv_sem):
    size_z, size_y, size_x, _ = f_ref.shape
    sizes = (size_x, size_y, size_z)
    reach = (widths[2], widths[1], widths[0])
    index = [lax.axis_index(a) for a in AXES]
    count = [lax.axis_size(a) for a in AXES]

    def exists(d):
        ok = True
        for a in range(3):
            if d[a] == -1:
                ok = jnp.logical_and(ok, index[a] > 0)
            elif d[a] == 1:
                ok = jnp.logical_and(ok, index[a] < count[a] - 1)
        return ok

    def device(d):
        return tuple(index[a] + d[a] for a in range(3))

    def source(a, step):
        s, w = sizes[a], reach[a]
        if step == -1:
            return slice(0, w)
        if step == 1:
            return slice(s - w, s)
        return slice(0, s)

    def side(a, step):
        s, w = sizes[a], reach[a]
        if step == -1:
            return slice(0, w)
        if step == 1:
            return slice(s + w, s + 2 * w)
        return slice(w, w + s)

    barrier = pltpu.get_barrier_semaphore()
    for d in DIRS:
        @pl.when(exists(d))
        def _():
            pl.semaphore_signal(barrier, inc=1, device_id=device(d), device_id_type=MESH)

    local = pltpu.make_async_copy(
        f_ref, p_ref.at[widths[0]:widths[0] + size_z, widths[1]:widths[1] + size_y,
                        widths[2]:widths[2] + size_x, :],
        local_sem.at[0])
    local.start()

    for d in DIRS:
        @pl.when(jnp.logical_not(exists(d)))
        def _():
            sx, sy, sz = (side(a, d[a]) for a in range(3))
            region = p_ref.at[sz, sy, sx, :]
            region[...] = jnp.zeros(region.shape, region.dtype)

    peers = 1
    for a in range(3):
        below = (index[a] + count[a] - 1) // count[a]
        above = (2 * count[a] - 2 - index[a]) // count[a]
        peers = peers * (1 + below + above)
    pl.semaphore_wait(barrier, peers - 1)

    copies = []
    for k, d in enumerate(DIRS):
        sx, sy, sz = (source(a, d[a]) for a in range(3))
        tx, ty, tz = (side(a, -d[a]) for a in range(3))
        copy = pltpu.make_async_remote_copy(
            src_ref=f_ref.at[sz, sy, sx, :],
            dst_ref=p_ref.at[tz, ty, tx, :],
            send_sem=send_sem.at[k],
            recv_sem=recv_sem.at[k],
            device_id=device(d),
            device_id_type=MESH,
        )
        copies.append((d, copy))

        @pl.when(exists(d))
        def _():
            copy.start()

    local.wait()
    for d, copy in copies:
        @pl.when(exists(d))
        def _():
            copy.wait_send()

        @pl.when(exists(tuple(-v for v in d)))
        def _():
            copy.wait_recv()


def with_rim(field, widths, collective_id):
    size_z, size_y, size_x, chans = field.shape
    return pl.pallas_call(
        functools.partial(rim_kernel, widths),
        out_shape=jax.ShapeDtypeStruct(
            (size_z + 2 * widths[0], size_y + 2 * widths[1], size_x + 2 * widths[2], chans),
            field.dtype),
        in_specs=[pl.BlockSpec(memory_space=pltpu.VMEM)],
        out_specs=pl.BlockSpec(memory_space=pltpu.VMEM),
        scratch_shapes=[
            pltpu.SemaphoreType.DMA((1,)),
            pltpu.SemaphoreType.DMA((len(DIRS),)),
            pltpu.SemaphoreType.DMA((len(DIRS),)),
        ],
        compiler_params=pltpu.CompilerParams(collective_id=collective_id, has_side_effects=True),
    )(field)


def region_mask(tissue, repeats, block_starts, extents, margin):
    padded = jnp.pad(tissue, 1)
    counts = [extents[d] // repeats[d] + 2 for d in range(3)]
    starts = [jnp.asarray(block_starts[d], dtype=jnp.int32) for d in range(3)]
    table = lax.dynamic_slice(padded, starts, counts)
    for d in range(3):
        table = jnp.repeat(table, repeats[d], axis=d)
    table = table[
        repeats[0] - margin : repeats[0] + extents[0] + margin,
        repeats[1] - margin : repeats[1] + extents[1] + margin,
        repeats[2] - margin : repeats[2] + extents[2] + margin,
    ]
    return table.astype(jnp.float32).transpose(2, 1, 0)[..., None]


def finish(summed, offsets, tissue_mask):
    return (jnp.maximum(summed + offsets, 0.0) * tissue_mask).astype(jnp.bfloat16)


def conv_taps(padded, weights):
    size_z = padded.shape[0] - 2
    stacked = jnp.concatenate([padded[k:k + size_z] for k in range(3)], axis=-1)
    kernel = weights.reshape(3, 3, 3, weights.shape[1], weights.shape[2]).transpose(1, 0, 2, 4, 3)
    kernel = kernel.reshape(3, 3, 3 * weights.shape[2], weights.shape[1])
    return lax.conv_general_dilated(
        stacked, kernel, (1, 1), "VALID",
        dimension_numbers=("NHWC", "HWIO", "NHWC"), preferred_element_type=jnp.float32)


def conv_cube(padded, weights):
    kernel = weights.reshape(3, 3, 3, weights.shape[1], weights.shape[2]).transpose(2, 1, 0, 4, 3)
    result = lax.conv_general_dilated(
        padded[None], kernel, (1, 1, 1), "VALID",
        dimension_numbers=("NDHWC", "DHWIO", "NDHWC"), preferred_element_type=jnp.float32)
    return result[0]


def down_first(grid, weights):
    channels, size_z, size_y, size_x = grid.shape
    split = grid.reshape(channels, size_z // 2, 2, size_y // 2, 2, size_x // 2, 2)
    grouped = weights.reshape(2, 2, 2, weights.shape[1], weights.shape[2])
    return jnp.einsum("abkoi,izkybxa->zyxo", grouped, split, preferred_element_type=jnp.float32)


def down_cells(field, weights):
    size_z, size_y, size_x, channels = field.shape
    split = field.reshape(size_z // 2, 2, size_y // 2, 2, size_x // 2, 2, channels)
    grouped = weights.reshape(2, 2, 2, weights.shape[1], weights.shape[2])
    return jnp.einsum("abkoi,zkybxai->zyxo", grouped, split, preferred_element_type=jnp.float32)


def packed(field):
    size_z, size_y, size_x, chans = field.shape
    return field.transpose(3, 0, 1, 2).reshape(chans, size_z, size_y * size_x)


def local(volume, tissue, w_down1, b_down1, w_conv1a, b_conv1a, w_conv1b, b_conv1b,
          w_down2, b_down2, w_conv2a, b_conv2a, w_conv2b, b_conv2b):
    index_x = lax.axis_index("gx")
    index_y = lax.axis_index("gy")
    index_z = lax.axis_index("gz")
    grid_zero = volume.reshape(volume.shape[0], volume.shape[1], CY, CX)
    first_x = CX // 2
    first_y = CY // 2
    first_z = volume.shape[1] // 2
    first_blocks = (index_x * (first_x // 4), index_y * (first_y // 4), index_z * (first_z // 8))
    mask_one = region_mask(tissue, (4, 4, 8), first_blocks, (first_x, first_y, first_z), 0)
    mask_one_wide = region_mask(tissue, (4, 4, 8), first_blocks, (first_x, first_y, first_z), 1)
    down_one = finish(down_first(grid_zero, w_down1), b_down1, mask_one)
    paired = down_one.reshape(first_z, first_y, first_x // 2, 2 * down_one.shape[3])
    rimmed = with_rim(paired, (2, 2, 2), 0)
    rimmed = rimmed.reshape(first_z + 4, first_y + 4, first_x + 8, down_one.shape[3])[:, :, 2:-2]
    inner_one = finish(conv_taps(rimmed, w_conv1a), b_conv1a, mask_one_wide)
    feat_one = finish(conv_taps(inner_one, w_conv1b), b_conv1b, mask_one)
    second_x = first_x // 2
    second_y = first_y // 2
    second_z = first_z // 2
    second_blocks = (index_x * (second_x // 2), index_y * (second_y // 2), index_z * (second_z // 4))
    mask_two = region_mask(tissue, (2, 2, 4), second_blocks, (second_x, second_y, second_z), 0)
    mask_two_wide = region_mask(tissue, (2, 2, 4), second_blocks, (second_x, second_y, second_z), 1)
    down_two = finish(down_cells(feat_one, w_down2), b_down2, mask_two)
    middle = finish(conv_cube(with_rim(down_two, (2, 2, 2), 1), w_conv2a), b_conv2a, mask_two_wide)
    feat_two = finish(conv_cube(middle, w_conv2b), b_conv2b, mask_two)
    return (packed(feat_one), packed(feat_two))


def solution(mesh):
    return jax.shard_map(
        local,
        mesh=mesh,
        in_specs=(P(None, "gz", ("gx", "gy")),) + (P(),) * 13,
        out_specs=(P(None, "gz", ("gx", "gy")), P(None, "gz", ("gx", "gy"))),
        check_vma=False,
    )
```

```python
import functools

import jax
import jax.numpy as jnp
from jax import lax
from jax.experimental import pallas as pl
from jax.experimental.pallas import tpu as pltpu
from jax.sharding import PartitionSpec as P

CX = 64
CY = 32
AXES = ("gx", "gy", "gz")
MESH = pl.DeviceIdType.MESH
DIRS = [
    (dx, dy, dz)
    for dx in (-1, 0, 1)
    for dy in (-1, 0, 1)
    for dz in (-1, 0, 1)
    if (dx, dy, dz) != (0, 0, 0)
]


def rim_kernel(width, f_ref, p_ref, local_sem, send_sem, recv_sem):
    size_z, size_y, size_x, _ = f_ref.shape
    sizes = (size_x, size_y, size_z)
    index = [lax.axis_index(a) for a in AXES]
    count = [lax.axis_size(a) for a in AXES]

    def exists(d):
        ok = True
        for a in range(3):
            if d[a] == -1:
                ok = jnp.logical_and(ok, index[a] > 0)
            elif d[a] == 1:
                ok = jnp.logical_and(ok, index[a] < count[a] - 1)
        return ok

    def device(d):
        return tuple(index[a] + d[a] for a in range(3))

    def source(a, step):
        s = sizes[a]
        if step == -1:
            return slice(0, width)
        if step == 1:
            return slice(s - width, s)
        return slice(0, s)

    def side(a, step):
        s = sizes[a]
        if step == -1:
            return slice(0, width)
        if step == 1:
            return slice(s + width, s + 2 * width)
        return slice(width, width + s)

    barrier = pltpu.get_barrier_semaphore()
    for d in DIRS:
        @pl.when(exists(d))
        def _():
            pl.semaphore_signal(barrier, inc=1, device_id=device(d), device_id_type=MESH)

    local = pltpu.make_async_copy(
        f_ref, p_ref.at[width:width + size_z, width:width + size_y, width:width + size_x, :],
        local_sem.at[0])
    local.start()

    for d in DIRS:
        @pl.when(jnp.logical_not(exists(d)))
        def _():
            sx, sy, sz = (side(a, d[a]) for a in range(3))
            region = p_ref.at[sz, sy, sx, :]
            region[...] = jnp.zeros(region.shape, region.dtype)

    peers = 1
    for a in range(3):
        below = (index[a] + count[a] - 1) // count[a]
        above = (2 * count[a] - 2 - index[a]) // count[a]
        peers = peers * (1 + below + above)
    pl.semaphore_wait(barrier, peers - 1)

    copies = []
    for k, d in enumerate(DIRS):
        sx, sy, sz = (source(a, d[a]) for a in range(3))
        tx, ty, tz = (side(a, -d[a]) for a in range(3))
        copy = pltpu.make_async_remote_copy(
            src_ref=f_ref.at[sz, sy, sx, :],
            dst_ref=p_ref.at[tz, ty, tx, :],
            send_sem=send_sem.at[k],
            recv_sem=recv_sem.at[k],
            device_id=device(d),
            device_id_type=MESH,
        )
        copies.append((d, copy))

        @pl.when(exists(d))
        def _():
            copy.start()

    local.wait()
    for d, copy in copies:
        @pl.when(exists(d))
        def _():
            copy.wait_send()

        @pl.when(exists(tuple(-v for v in d)))
        def _():
            copy.wait_recv()


def with_rim(field, width, collective_id):
    size_z, size_y, size_x, chans = field.shape
    return pl.pallas_call(
        functools.partial(rim_kernel, width),
        out_shape=jax.ShapeDtypeStruct(
            (size_z + 2 * width, size_y + 2 * width, size_x + 2 * width, chans), field.dtype),
        in_specs=[pl.BlockSpec(memory_space=pltpu.VMEM)],
        out_specs=pl.BlockSpec(memory_space=pltpu.VMEM),
        scratch_shapes=[
            pltpu.SemaphoreType.DMA((1,)),
            pltpu.SemaphoreType.DMA((len(DIRS),)),
            pltpu.SemaphoreType.DMA((len(DIRS),)),
        ],
        compiler_params=pltpu.CompilerParams(collective_id=collective_id, has_side_effects=True),
    )(field)


def region_mask(tissue, repeats, block_starts, extents, margin):
    padded = jnp.pad(tissue, 1)
    counts = [extents[d] // repeats[d] + 2 for d in range(3)]
    starts = [jnp.asarray(block_starts[d], dtype=jnp.int32) for d in range(3)]
    table = lax.dynamic_slice(padded, starts, counts)
    for d in range(3):
        table = jnp.repeat(table, repeats[d], axis=d)
    table = table[
        repeats[0] - margin : repeats[0] + extents[0] + margin,
        repeats[1] - margin : repeats[1] + extents[1] + margin,
        repeats[2] - margin : repeats[2] + extents[2] + margin,
    ]
    return table.astype(jnp.float32).transpose(2, 1, 0)[..., None]


def finish(summed, offsets, tissue_mask):
    return (jnp.maximum(summed + offsets, 0.0) * tissue_mask).astype(jnp.bfloat16)


def conv_taps(padded, weights):
    size_z = padded.shape[0] - 2
    stacked = jnp.concatenate([padded[k:k + size_z] for k in range(3)], axis=-1)
    kernel = weights.reshape(3, 3, 3, weights.shape[1], weights.shape[2]).transpose(1, 0, 2, 4, 3)
    kernel = kernel.reshape(3, 3, 3 * weights.shape[2], weights.shape[1])
    return lax.conv_general_dilated(
        stacked, kernel, (1, 1), "VALID",
        dimension_numbers=("NHWC", "HWIO", "NHWC"), preferred_element_type=jnp.float32)


def conv_cube(padded, weights):
    kernel = weights.reshape(3, 3, 3, weights.shape[1], weights.shape[2]).transpose(2, 1, 0, 4, 3)
    result = lax.conv_general_dilated(
        padded[None], kernel, (1, 1, 1), "VALID",
        dimension_numbers=("NDHWC", "DHWIO", "NDHWC"), preferred_element_type=jnp.float32)
    return result[0]


def down_first(grid, weights):
    grouped = weights.reshape(2, 2, 2, weights.shape[1], weights.shape[2])
    total = None
    for k in range(2):
        kernel = grouped[:, :, k].transpose(1, 0, 3, 2)
        term = lax.conv_general_dilated(
            grid[:, k::2], kernel, (2, 2), "VALID",
            dimension_numbers=("CNHW", "HWIO", "NHWC"), preferred_element_type=jnp.float32)
        total = term if total is None else total + term
    return total


def down_cells(field, weights):
    size_z, size_y, size_x, channels = field.shape
    split = field.reshape(size_z // 2, 2, size_y // 2, 2, size_x // 2, 2, channels)
    grouped = weights.reshape(2, 2, 2, weights.shape[1], weights.shape[2])
    return jnp.einsum("abkoi,zkybxai->zyxo", grouped, split, preferred_element_type=jnp.float32)


def packed(field):
    size_z, size_y, size_x, chans = field.shape
    return field.transpose(3, 0, 1, 2).reshape(chans, size_z, size_y * size_x)


def local(volume, tissue, w_down1, b_down1, w_conv1a, b_conv1a, w_conv1b, b_conv1b,
          w_down2, b_down2, w_conv2a, b_conv2a, w_conv2b, b_conv2b):
    index_x = lax.axis_index("gx")
    index_y = lax.axis_index("gy")
    index_z = lax.axis_index("gz")
    grid_zero = volume.reshape(volume.shape[0], volume.shape[1], CY, CX)
    first_x = CX // 2
    first_y = CY // 2
    first_z = volume.shape[1] // 2
    first_blocks = (index_x * (first_x // 4), index_y * (first_y // 4), index_z * (first_z // 8))
    mask_one = region_mask(tissue, (4, 4, 8), first_blocks, (first_x, first_y, first_z), 0)
    mask_one_wide = region_mask(tissue, (4, 4, 8), first_blocks, (first_x, first_y, first_z), 1)
    down_one = finish(down_first(grid_zero, w_down1), b_down1, mask_one)
    inner_one = finish(conv_taps(with_rim(down_one, 2, 0), w_conv1a), b_conv1a, mask_one_wide)
    feat_one = finish(conv_taps(inner_one, w_conv1b), b_conv1b, mask_one)
    second_x = first_x // 2
    second_y = first_y // 2
    second_z = first_z // 2
    second_blocks = (index_x * (second_x // 2), index_y * (second_y // 2), index_z * (second_z // 4))
    mask_two = region_mask(tissue, (2, 2, 4), second_blocks, (second_x, second_y, second_z), 0)
    mask_two_wide = region_mask(tissue, (2, 2, 4), second_blocks, (second_x, second_y, second_z), 1)
    down_two = finish(down_cells(feat_one, w_down2), b_down2, mask_two)
    middle = finish(conv_cube(with_rim(down_two, 2, 1), w_conv2a), b_conv2a, mask_two_wide)
    feat_two = finish(conv_cube(middle, w_conv2b), b_conv2b, mask_two)
    return (packed(feat_one), packed(feat_two))


def solution(mesh):
    return jax.shard_map(
        local,
        mesh=mesh,
        in_specs=(P(None, "gz", ("gx", "gy")),) + (P(),) * 13,
        out_specs=(P(None, "gz", ("gx", "gy")), P(None, "gz", ("gx", "gy"))),
        check_vma=False,
    )
```

```python
import functools

import jax
import jax.numpy as jnp
from jax import lax
from jax.experimental import pallas as pl
from jax.experimental.pallas import tpu as pltpu
from jax.sharding import PartitionSpec as P

CX = 64
CY = 32
AXES = ("gx", "gy", "gz")
MESH = pl.DeviceIdType.MESH
DIRS = [
    (dx, dy, dz)
    for dx in (-1, 0, 1)
    for dy in (-1, 0, 1)
    for dz in (-1, 0, 1)
    if (dx, dy, dz) != (0, 0, 0)
]


def rim_kernel(width, stack, f_ref, *refs):
    if stack:
        s_ref, p_ref, local_sem, send_sem, recv_sem = refs
    else:
        p_ref, local_sem, send_sem, recv_sem = refs
    size_z, size_y, size_x, _ = f_ref.shape
    sizes = (size_x, size_y, size_z)
    index = [lax.axis_index(a) for a in AXES]
    count = [lax.axis_size(a) for a in AXES]

    def exists(d):
        ok = True
        for a in range(3):
            if d[a] == -1:
                ok = jnp.logical_and(ok, index[a] > 0)
            elif d[a] == 1:
                ok = jnp.logical_and(ok, index[a] < count[a] - 1)
        return ok

    def device(d):
        return tuple(index[a] + d[a] for a in range(3))

    def source(a, step):
        s = sizes[a]
        if step == -1:
            return slice(0, width)
        if step == 1:
            return slice(s - width, s)
        return slice(0, s)

    def side(a, step):
        s = sizes[a]
        if step == -1:
            return slice(0, width)
        if step == 1:
            return slice(s + width, s + 2 * width)
        return slice(width, width + s)

    barrier = pltpu.get_barrier_semaphore()
    for d in DIRS:
        @pl.when(exists(d))
        def _():
            pl.semaphore_signal(barrier, inc=1, device_id=device(d), device_id_type=MESH)

    local = pltpu.make_async_copy(
        f_ref, p_ref.at[width:width + size_z, width:width + size_y, width:width + size_x, :],
        local_sem.at[0])
    local.start()

    for d in DIRS:
        @pl.when(jnp.logical_not(exists(d)))
        def _():
            sx, sy, sz = (side(a, d[a]) for a in range(3))
            region = p_ref.at[sz, sy, sx, :]
            region[...] = jnp.zeros(region.shape, region.dtype)

    peers = 1
    for a in range(3):
        below = (index[a] + count[a] - 1) // count[a]
        above = (2 * count[a] - 2 - index[a]) // count[a]
        peers = peers * (1 + below + above)
    pl.semaphore_wait(barrier, peers - 1)

    copies = []
    for k, d in enumerate(DIRS):
        sx, sy, sz = (source(a, d[a]) for a in range(3))
        tx, ty, tz = (side(a, -d[a]) for a in range(3))
        copy = pltpu.make_async_remote_copy(
            src_ref=f_ref.at[sz, sy, sx, :],
            dst_ref=p_ref.at[tz, ty, tx, :],
            send_sem=send_sem.at[k],
            recv_sem=recv_sem.at[k],
            device_id=device(d),
            device_id_type=MESH,
        )
        copies.append((d, copy))

        @pl.when(exists(d))
        def _():
            copy.start()

    local.wait()
    for d, copy in copies:
        @pl.when(exists(d))
        def _():
            copy.wait_send()

        @pl.when(exists(tuple(-v for v in d)))
        def _():
            copy.wait_recv()

    if stack:
        chans = f_ref.shape[3]
        depth = s_ref.shape[0]
        for k in range(3):
            s_ref[:, :, :, k * chans:(k + 1) * chans] = p_ref[k:k + depth]


def with_rim(field, width, collective_id, stack):
    size_z, size_y, size_x, chans = field.shape
    padded = (size_z + 2 * width, size_y + 2 * width, size_x + 2 * width, chans)
    sems = [
        pltpu.SemaphoreType.DMA((1,)),
        pltpu.SemaphoreType.DMA((len(DIRS),)),
        pltpu.SemaphoreType.DMA((len(DIRS),)),
    ]
    if stack:
        shape = (padded[0] - 2, padded[1], padded[2], 3 * chans)
        scratch = [pltpu.VMEM(padded, field.dtype)] + sems
    else:
        shape = padded
        scratch = sems
    return pl.pallas_call(
        functools.partial(rim_kernel, width, stack),
        out_shape=jax.ShapeDtypeStruct(shape, field.dtype),
        in_specs=[pl.BlockSpec(memory_space=pltpu.VMEM)],
        out_specs=pl.BlockSpec(memory_space=pltpu.VMEM),
        scratch_shapes=scratch,
        compiler_params=pltpu.CompilerParams(collective_id=collective_id, has_side_effects=True),
    )(field)


def conv_stacked(stacked, weights):
    kernel = weights.reshape(3, 3, 3, weights.shape[1], weights.shape[2]).transpose(1, 0, 2, 4, 3)
    kernel = kernel.reshape(3, 3, 3 * weights.shape[2], weights.shape[1])
    return lax.conv_general_dilated(
        stacked, kernel, (1, 1), "VALID",
        dimension_numbers=("NHWC", "HWIO", "NHWC"), preferred_element_type=jnp.float32)


def region_mask(tissue, repeats, block_starts, extents, margin):
    padded = jnp.pad(tissue, 1)
    counts = [extents[d] // repeats[d] + 2 for d in range(3)]
    starts = [jnp.asarray(block_starts[d], dtype=jnp.int32) for d in range(3)]
    table = lax.dynamic_slice(padded, starts, counts)
    for d in range(3):
        table = jnp.repeat(table, repeats[d], axis=d)
    table = table[
        repeats[0] - margin : repeats[0] + extents[0] + margin,
        repeats[1] - margin : repeats[1] + extents[1] + margin,
        repeats[2] - margin : repeats[2] + extents[2] + margin,
    ]
    return table.astype(jnp.float32).transpose(2, 1, 0)[..., None]


def finish(summed, offsets, tissue_mask):
    return (jnp.maximum(summed + offsets, 0.0) * tissue_mask).astype(jnp.bfloat16)


def conv_taps(padded, weights):
    size_z = padded.shape[0] - 2
    stacked = jnp.concatenate([padded[k:k + size_z] for k in range(3)], axis=-1)
    kernel = weights.reshape(3, 3, 3, weights.shape[1], weights.shape[2]).transpose(1, 0, 2, 4, 3)
    kernel = kernel.reshape(3, 3, 3 * weights.shape[2], weights.shape[1])
    return lax.conv_general_dilated(
        stacked, kernel, (1, 1), "VALID",
        dimension_numbers=("NHWC", "HWIO", "NHWC"), preferred_element_type=jnp.float32)


def conv_cube(padded, weights):
    kernel = weights.reshape(3, 3, 3, weights.shape[1], weights.shape[2]).transpose(2, 1, 0, 4, 3)
    result = lax.conv_general_dilated(
        padded[None], kernel, (1, 1, 1), "VALID",
        dimension_numbers=("NDHWC", "DHWIO", "NDHWC"), preferred_element_type=jnp.float32)
    return result[0]


def down_first(grid, weights):
    channels, size_z, size_y, size_x = grid.shape
    split = grid.reshape(channels, size_z // 2, 2, size_y // 2, 2, size_x // 2, 2)
    grouped = weights.reshape(2, 2, 2, weights.shape[1], weights.shape[2])
    return jnp.einsum("abkoi,izkybxa->zyxo", grouped, split, preferred_element_type=jnp.float32)


def down_cells(field, weights):
    size_z, size_y, size_x, channels = field.shape
    split = field.reshape(size_z // 2, 2, size_y // 2, 2, size_x // 2, 2, channels)
    grouped = weights.reshape(2, 2, 2, weights.shape[1], weights.shape[2])
    return jnp.einsum("abkoi,zkybxai->zyxo", grouped, split, preferred_element_type=jnp.float32)


def packed(field):
    size_z, size_y, size_x, chans = field.shape
    return field.transpose(3, 0, 1, 2).reshape(chans, size_z, size_y * size_x)


def local(volume, tissue, w_down1, b_down1, w_conv1a, b_conv1a, w_conv1b, b_conv1b,
          w_down2, b_down2, w_conv2a, b_conv2a, w_conv2b, b_conv2b):
    index_x = lax.axis_index("gx")
    index_y = lax.axis_index("gy")
    index_z = lax.axis_index("gz")
    grid_zero = volume.reshape(volume.shape[0], volume.shape[1], CY, CX)
    first_x = CX // 2
    first_y = CY // 2
    first_z = volume.shape[1] // 2
    first_blocks = (index_x * (first_x // 4), index_y * (first_y // 4), index_z * (first_z // 8))
    mask_one = region_mask(tissue, (4, 4, 8), first_blocks, (first_x, first_y, first_z), 0)
    mask_one_wide = region_mask(tissue, (4, 4, 8), first_blocks, (first_x, first_y, first_z), 1)
    down_one = finish(down_first(grid_zero, w_down1), b_down1, mask_one)
    inner_one = finish(conv_stacked(with_rim(down_one, 2, 0, True), w_conv1a), b_conv1a, mask_one_wide)
    feat_one = finish(conv_taps(inner_one, w_conv1b), b_conv1b, mask_one)
    second_x = first_x // 2
    second_y = first_y // 2
    second_z = first_z // 2
    second_blocks = (index_x * (second_x // 2), index_y * (second_y // 2), index_z * (second_z // 4))
    mask_two = region_mask(tissue, (2, 2, 4), second_blocks, (second_x, second_y, second_z), 0)
    mask_two_wide = region_mask(tissue, (2, 2, 4), second_blocks, (second_x, second_y, second_z), 1)
    down_two = finish(down_cells(feat_one, w_down2), b_down2, mask_two)
    middle = finish(conv_cube(with_rim(down_two, 2, 1, False), w_conv2a), b_conv2a, mask_two_wide)
    feat_two = finish(conv_cube(middle, w_conv2b), b_conv2b, mask_two)
    return (packed(feat_one), packed(feat_two))


def solution(mesh):
    return jax.shard_map(
        local,
        mesh=mesh,
        in_specs=(P(None, "gz", ("gx", "gy")),) + (P(),) * 13,
        out_specs=(P(None, "gz", ("gx", "gy")), P(None, "gz", ("gx", "gy"))),
        check_vma=False,
    )
```

```python
import functools

import jax
import jax.numpy as jnp
from jax import lax
from jax.experimental import pallas as pl
from jax.experimental.pallas import tpu as pltpu
from jax.sharding import PartitionSpec as P

CX = 64
CY = 32
AXES = ("gx", "gy", "gz")
MESH = pl.DeviceIdType.MESH
DIRS = [
    (dx, dy, dz)
    for dx in (-1, 0, 1)
    for dy in (-1, 0, 1)
    for dz in (-1, 0, 1)
    if (dx, dy, dz) != (0, 0, 0)
]


def rim_kernel(width, stack, f_ref, *refs):
    if stack:
        s_ref, p_ref, local_sem, send_sem, recv_sem = refs
    else:
        p_ref, local_sem, send_sem, recv_sem = refs
    size_z, size_y, size_x, _ = f_ref.shape
    sizes = (size_x, size_y, size_z)
    index = [lax.axis_index(a) for a in AXES]
    count = [lax.axis_size(a) for a in AXES]

    def exists(d):
        ok = True
        for a in range(3):
            if d[a] == -1:
                ok = jnp.logical_and(ok, index[a] > 0)
            elif d[a] == 1:
                ok = jnp.logical_and(ok, index[a] < count[a] - 1)
        return ok

    def device(d):
        return tuple(index[a] + d[a] for a in range(3))

    def source(a, step):
        s = sizes[a]
        if step == -1:
            return slice(0, width)
        if step == 1:
            return slice(s - width, s)
        return slice(0, s)

    def side(a, step):
        s = sizes[a]
        if step == -1:
            return slice(0, width)
        if step == 1:
            return slice(s + width, s + 2 * width)
        return slice(width, width + s)

    barrier = pltpu.get_barrier_semaphore()
    for d in DIRS:
        @pl.when(exists(d))
        def _():
            pl.semaphore_signal(barrier, inc=1, device_id=device(d), device_id_type=MESH)

    local = pltpu.make_async_copy(
        f_ref, p_ref.at[width:width + size_z, width:width + size_y, width:width + size_x, :],
        local_sem.at[0])
    local.start()

    for d in DIRS:
        @pl.when(jnp.logical_not(exists(d)))
        def _():
            sx, sy, sz = (side(a, d[a]) for a in range(3))
            region = p_ref.at[sz, sy, sx, :]
            region[...] = jnp.zeros(region.shape, region.dtype)

    peers = 1
    for a in range(3):
        below = (index[a] + count[a] - 1) // count[a]
        above = (2 * count[a] - 2 - index[a]) // count[a]
        peers = peers * (1 + below + above)
    pl.semaphore_wait(barrier, peers - 1)

    copies = []
    for k, d in enumerate(DIRS):
        sx, sy, sz = (source(a, d[a]) for a in range(3))
        tx, ty, tz = (side(a, -d[a]) for a in range(3))
        copy = pltpu.make_async_remote_copy(
            src_ref=f_ref.at[sz, sy, sx, :],
            dst_ref=p_ref.at[tz, ty, tx, :],
            send_sem=send_sem.at[k],
            recv_sem=recv_sem.at[k],
            device_id=device(d),
            device_id_type=MESH,
        )
        copies.append((d, copy))

        @pl.when(exists(d))
        def _():
            copy.start()

    local.wait()
    for d, copy in copies:
        @pl.when(exists(d))
        def _():
            copy.wait_send()

        @pl.when(exists(tuple(-v for v in d)))
        def _():
            copy.wait_recv()

    if stack:
        chans = f_ref.shape[3]
        depth = s_ref.shape[0]
        for k in range(3):
            s_ref[:, :, :, k * chans:(k + 1) * chans] = p_ref[k:k + depth]


def with_rim(field, width, collective_id, stack):
    size_z, size_y, size_x, chans = field.shape
    padded = (size_z + 2 * width, size_y + 2 * width, size_x + 2 * width, chans)
    sems = [
        pltpu.SemaphoreType.DMA((1,)),
        pltpu.SemaphoreType.DMA((len(DIRS),)),
        pltpu.SemaphoreType.DMA((len(DIRS),)),
    ]
    if stack:
        shape = (padded[0] - 2, padded[1], padded[2], 3 * chans)
        scratch = [pltpu.VMEM(padded, field.dtype)] + sems
    else:
        shape = padded
        scratch = sems
    return pl.pallas_call(
        functools.partial(rim_kernel, width, stack),
        out_shape=jax.ShapeDtypeStruct(shape, field.dtype),
        in_specs=[pl.BlockSpec(memory_space=pltpu.VMEM)],
        out_specs=pl.BlockSpec(memory_space=pltpu.VMEM),
        scratch_shapes=scratch,
        compiler_params=pltpu.CompilerParams(collective_id=collective_id, has_side_effects=True),
    )(field)


def conv_stacked(stacked, weights):
    kernel = weights.reshape(3, 3, 3, weights.shape[1], weights.shape[2]).transpose(0, 1, 3, 2, 4)
    kernel = kernel.reshape(3, 3, weights.shape[1], 3 * weights.shape[2])
    return lax.conv_general_dilated(
        stacked, kernel, (1, 1), "VALID",
        dimension_numbers=("NHWC", "WHOI", "NHWC"), preferred_element_type=jnp.float32)


def region_mask(tissue, repeats, block_starts, extents, margin):
    padded = jnp.pad(tissue, 1)
    counts = [extents[d] // repeats[d] + 2 for d in range(3)]
    starts = [jnp.asarray(block_starts[d], dtype=jnp.int32) for d in range(3)]
    table = lax.dynamic_slice(padded, starts, counts)
    for d in range(3):
        table = jnp.repeat(table, repeats[d], axis=d)
    table = table[
        repeats[0] - margin : repeats[0] + extents[0] + margin,
        repeats[1] - margin : repeats[1] + extents[1] + margin,
        repeats[2] - margin : repeats[2] + extents[2] + margin,
    ]
    return table.astype(jnp.float32).transpose(2, 1, 0)[..., None]


def finish(summed, offsets, tissue_mask):
    return (jnp.maximum(summed + offsets, 0.0) * tissue_mask).astype(jnp.bfloat16)


def conv_taps(padded, weights):
    size_z = padded.shape[0] - 2
    stacked = jnp.concatenate([padded[k:k + size_z] for k in range(3)], axis=-1)
    kernel = weights.reshape(3, 3, 3, weights.shape[1], weights.shape[2]).transpose(0, 1, 3, 2, 4)
    kernel = kernel.reshape(3, 3, weights.shape[1], 3 * weights.shape[2])
    return lax.conv_general_dilated(
        stacked, kernel, (1, 1), "VALID",
        dimension_numbers=("NHWC", "WHOI", "NHWC"), preferred_element_type=jnp.float32)


def conv_cube(padded, weights):
    kernel = weights.reshape(3, 3, 3, weights.shape[1], weights.shape[2]).transpose(2, 1, 0, 4, 3)
    result = lax.conv_general_dilated(
        padded[None], kernel, (1, 1, 1), "VALID",
        dimension_numbers=("NDHWC", "DHWIO", "NDHWC"), preferred_element_type=jnp.float32)
    return result[0]


def down_first(grid, weights):
    channels, size_z, size_y, size_x = grid.shape
    split = grid.reshape(channels, size_z // 2, 2, size_y // 2, 2, size_x // 2, 2)
    grouped = weights.reshape(2, 2, 2, weights.shape[1], weights.shape[2])
    return jnp.einsum("abkoi,izkybxa->zyxo", grouped, split, preferred_element_type=jnp.float32)


def down_cells(field, weights):
    size_z, size_y, size_x, channels = field.shape
    split = field.reshape(size_z // 2, 2, size_y // 2, 2, size_x // 2, 2, channels)
    grouped = weights.reshape(2, 2, 2, weights.shape[1], weights.shape[2])
    return jnp.einsum("abkoi,zkybxai->zyxo", grouped, split, preferred_element_type=jnp.float32)


def packed(field):
    size_z, size_y, size_x, chans = field.shape
    return field.transpose(3, 0, 1, 2).reshape(chans, size_z, size_y * size_x)


def local(volume, tissue, w_down1, b_down1, w_conv1a, b_conv1a, w_conv1b, b_conv1b,
          w_down2, b_down2, w_conv2a, b_conv2a, w_conv2b, b_conv2b):
    index_x = lax.axis_index("gx")
    index_y = lax.axis_index("gy")
    index_z = lax.axis_index("gz")
    grid_zero = volume.reshape(volume.shape[0], volume.shape[1], CY, CX)
    first_x = CX // 2
    first_y = CY // 2
    first_z = volume.shape[1] // 2
    first_blocks = (index_x * (first_x // 4), index_y * (first_y // 4), index_z * (first_z // 8))
    mask_one = region_mask(tissue, (4, 4, 8), first_blocks, (first_x, first_y, first_z), 0)
    mask_one_wide = region_mask(tissue, (4, 4, 8), first_blocks, (first_x, first_y, first_z), 1)
    down_one = finish(down_first(grid_zero, w_down1), b_down1, mask_one)
    inner_one = finish(conv_stacked(with_rim(down_one, 2, 0, True), w_conv1a), b_conv1a, mask_one_wide)
    feat_one = finish(conv_taps(inner_one, w_conv1b), b_conv1b, mask_one)
    second_x = first_x // 2
    second_y = first_y // 2
    second_z = first_z // 2
    second_blocks = (index_x * (second_x // 2), index_y * (second_y // 2), index_z * (second_z // 4))
    mask_two = region_mask(tissue, (2, 2, 4), second_blocks, (second_x, second_y, second_z), 0)
    mask_two_wide = region_mask(tissue, (2, 2, 4), second_blocks, (second_x, second_y, second_z), 1)
    down_two = finish(down_cells(feat_one, w_down2), b_down2, mask_two)
    middle = finish(conv_cube(with_rim(down_two, 2, 1, False), w_conv2a), b_conv2a, mask_two_wide)
    feat_two = finish(conv_cube(middle, w_conv2b), b_conv2b, mask_two)
    return (packed(feat_one), packed(feat_two))


def solution(mesh):
    return jax.shard_map(
        local,
        mesh=mesh,
        in_specs=(P(None, "gz", ("gx", "gy")),) + (P(),) * 13,
        out_specs=(P(None, "gz", ("gx", "gy")), P(None, "gz", ("gx", "gy"))),
        check_vma=False,
    )
```

```python
import functools

import jax
import jax.numpy as jnp
from jax import lax
from jax.experimental import pallas as pl
from jax.experimental.pallas import tpu as pltpu
from jax.sharding import PartitionSpec as P

CX = 64
CY = 32
AXES = ("gx", "gy", "gz")
MESH = pl.DeviceIdType.MESH
DIRS = [
    (dx, dy, dz)
    for dx in (-1, 0, 1)
    for dy in (-1, 0, 1)
    for dz in (-1, 0, 1)
    if (dx, dy, dz) != (0, 0, 0)
]


def rim_kernel(width, stack, f_ref, *refs):
    if stack:
        s_ref, p_ref, local_sem, send_sem, recv_sem = refs
    else:
        p_ref, local_sem, send_sem, recv_sem = refs
    size_z, size_y, size_x, _ = f_ref.shape
    sizes = (size_x, size_y, size_z)
    index = [lax.axis_index(a) for a in AXES]
    count = [lax.axis_size(a) for a in AXES]

    def exists(d):
        ok = True
        for a in range(3):
            if d[a] == -1:
                ok = jnp.logical_and(ok, index[a] > 0)
            elif d[a] == 1:
                ok = jnp.logical_and(ok, index[a] < count[a] - 1)
        return ok

    def device(d):
        return tuple(index[a] + d[a] for a in range(3))

    def source(a, step):
        s = sizes[a]
        if step == -1:
            return slice(0, width)
        if step == 1:
            return slice(s - width, s)
        return slice(0, s)

    def side(a, step):
        s = sizes[a]
        if step == -1:
            return slice(0, width)
        if step == 1:
            return slice(s + width, s + 2 * width)
        return slice(width, width + s)

    barrier = pltpu.get_barrier_semaphore()
    for d in DIRS:
        @pl.when(exists(d))
        def _():
            pl.semaphore_signal(barrier, inc=1, device_id=device(d), device_id_type=MESH)

    local = pltpu.make_async_copy(
        f_ref, p_ref.at[width:width + size_z, width:width + size_y, width:width + size_x, :],
        local_sem.at[0])
    local.start()

    for d in DIRS:
        @pl.when(jnp.logical_not(exists(d)))
        def _():
            sx, sy, sz = (side(a, d[a]) for a in range(3))
            region = p_ref.at[sz, sy, sx, :]
            region[...] = jnp.zeros(region.shape, region.dtype)

    peers = 1
    for a in range(3):
        below = (index[a] + count[a] - 1) // count[a]
        above = (2 * count[a] - 2 - index[a]) // count[a]
        peers = peers * (1 + below + above)
    pl.semaphore_wait(barrier, peers - 1)

    copies = []
    for k, d in enumerate(DIRS):
        sx, sy, sz = (source(a, d[a]) for a in range(3))
        tx, ty, tz = (side(a, -d[a]) for a in range(3))
        copy = pltpu.make_async_remote_copy(
            src_ref=f_ref.at[sz, sy, sx, :],
            dst_ref=p_ref.at[tz, ty, tx, :],
            send_sem=send_sem.at[k],
            recv_sem=recv_sem.at[k],
            device_id=device(d),
            device_id_type=MESH,
        )
        copies.append((d, copy))

        @pl.when(exists(d))
        def _():
            copy.start()

    local.wait()
    for d, copy in copies:
        @pl.when(exists(d))
        def _():
            copy.wait_send()

        @pl.when(exists(tuple(-v for v in d)))
        def _():
            copy.wait_recv()

    if stack:
        chans = f_ref.shape[3]
        depth = s_ref.shape[0]
        for k in range(3):
            s_ref[:, :, :, k * chans:(k + 1) * chans] = p_ref[k:k + depth]


def with_rim(field, width, collective_id, stack):
    size_z, size_y, size_x, chans = field.shape
    padded = (size_z + 2 * width, size_y + 2 * width, size_x + 2 * width, chans)
    sems = [
        pltpu.SemaphoreType.DMA((1,)),
        pltpu.SemaphoreType.DMA((len(DIRS),)),
        pltpu.SemaphoreType.DMA((len(DIRS),)),
    ]
    if stack:
        shape = (padded[0] - 2, padded[1], padded[2], 3 * chans)
        scratch = [pltpu.VMEM(padded, field.dtype)] + sems
    else:
        shape = padded
        scratch = sems
    return pl.pallas_call(
        functools.partial(rim_kernel, width, stack),
        out_shape=jax.ShapeDtypeStruct(shape, field.dtype),
        in_specs=[pl.BlockSpec(memory_space=pltpu.VMEM)],
        out_specs=pl.BlockSpec(memory_space=pltpu.VMEM),
        scratch_shapes=scratch,
        compiler_params=pltpu.CompilerParams(collective_id=collective_id, has_side_effects=True),
    )(field)


def rim_any_kernel(width, owners, f_ref, p_ref, local_sem, send_sem, recv_sem):
    sizes = f_ref.shape[:3]
    index = [lax.axis_index(a) for a in AXES]
    count = [lax.axis_size(a) for a in AXES]

    def exists(d):
        ok = True
        for a in range(3):
            if d[a] == -1:
                ok = jnp.logical_and(ok, index[a] > 0)
            elif d[a] == 1:
                ok = jnp.logical_and(ok, index[a] < count[a] - 1)
        return ok

    def device(d):
        return tuple(index[a] + d[a] for a in range(3))

    def source(k, step):
        s = sizes[k]
        if step == -1:
            return slice(0, width)
        if step == 1:
            return slice(s - width, s)
        return slice(0, s)

    def side(k, step):
        s = sizes[k]
        if step == -1:
            return slice(0, width)
        if step == 1:
            return slice(s + width, s + 2 * width)
        return slice(width, width + s)

    def window(pick, d, sign):
        return tuple(pick(k, sign * d[owners[k]]) for k in range(3)) + (slice(None),)

    barrier = pltpu.get_barrier_semaphore()
    for d in DIRS:
        @pl.when(exists(d))
        def _():
            pl.semaphore_signal(barrier, inc=1, device_id=device(d), device_id_type=MESH)

    interior = tuple(slice(width, width + sizes[k]) for k in range(3)) + (slice(None),)
    local = pltpu.make_async_copy(f_ref, p_ref.at[interior], local_sem.at[0])
    local.start()

    for d in DIRS:
        @pl.when(jnp.logical_not(exists(d)))
        def _():
            region = p_ref.at[window(side, d, 1)]
            region[...] = jnp.zeros(region.shape, region.dtype)

    peers = 1
    for a in range(3):
        below = (index[a] + count[a] - 1) // count[a]
        above = (2 * count[a] - 2 - index[a]) // count[a]
        peers = peers * (1 + below + above)
    pl.semaphore_wait(barrier, peers - 1)

    copies = []
    for k, d in enumerate(DIRS):
        copy = pltpu.make_async_remote_copy(
            src_ref=f_ref.at[window(source, d, 1)],
            dst_ref=p_ref.at[window(side, d, -1)],
            send_sem=send_sem.at[k],
            recv_sem=recv_sem.at[k],
            device_id=device(d),
            device_id_type=MESH,
        )
        copies.append((d, copy))

        @pl.when(exists(d))
        def _():
            copy.start()

    local.wait()
    for d, copy in copies:
        @pl.when(exists(d))
        def _():
            copy.wait_send()

        @pl.when(exists(tuple(-v for v in d)))
        def _():
            copy.wait_recv()


def with_rim_any(field, width, owners, collective_id):
    sizes = field.shape[:3]
    return pl.pallas_call(
        functools.partial(rim_any_kernel, width, owners),
        out_shape=jax.ShapeDtypeStruct(
            tuple(s + 2 * width for s in sizes) + (field.shape[3],), field.dtype),
        in_specs=[pl.BlockSpec(memory_space=pltpu.VMEM)],
        out_specs=pl.BlockSpec(memory_space=pltpu.VMEM),
        scratch_shapes=[
            pltpu.SemaphoreType.DMA((1,)),
            pltpu.SemaphoreType.DMA((len(DIRS),)),
            pltpu.SemaphoreType.DMA((len(DIRS),)),
        ],
        compiler_params=pltpu.CompilerParams(collective_id=collective_id, has_side_effects=True),
    )(field)


def rim_yxz(field, width, collective_id):
    rimmed = with_rim_any(field.transpose(1, 2, 0, 3), width, (1, 0, 2), collective_id)
    return rimmed.transpose(2, 0, 1, 3)


def conv_stacked(stacked, weights):
    kernel = weights.reshape(3, 3, 3, weights.shape[1], weights.shape[2]).transpose(1, 0, 2, 4, 3)
    kernel = kernel.reshape(3, 3, 3 * weights.shape[2], weights.shape[1])
    return lax.conv_general_dilated(
        stacked, kernel, (1, 1), "VALID",
        dimension_numbers=("NHWC", "HWIO", "NHWC"), preferred_element_type=jnp.float32)


def region_mask(tissue, repeats, block_starts, extents, margin):
    padded = jnp.pad(tissue, 1)
    counts = [extents[d] // repeats[d] + 2 for d in range(3)]
    starts = [jnp.asarray(block_starts[d], dtype=jnp.int32) for d in range(3)]
    table = lax.dynamic_slice(padded, starts, counts)
    for d in range(3):
        table = jnp.repeat(table, repeats[d], axis=d)
    table = table[
        repeats[0] - margin : repeats[0] + extents[0] + margin,
        repeats[1] - margin : repeats[1] + extents[1] + margin,
        repeats[2] - margin : repeats[2] + extents[2] + margin,
    ]
    return table.astype(jnp.float32).transpose(2, 1, 0)[..., None]


def finish(summed, offsets, tissue_mask):
    return (jnp.maximum(summed + offsets, 0.0) * tissue_mask).astype(jnp.bfloat16)


def conv_taps(padded, weights):
    size_z = padded.shape[0] - 2
    stacked = jnp.concatenate([padded[k:k + size_z] for k in range(3)], axis=-1)
    kernel = weights.reshape(3, 3, 3, weights.shape[1], weights.shape[2]).transpose(1, 0, 2, 4, 3)
    kernel = kernel.reshape(3, 3, 3 * weights.shape[2], weights.shape[1])
    return lax.conv_general_dilated(
        stacked, kernel, (1, 1), "VALID",
        dimension_numbers=("NHWC", "HWIO", "NHWC"), preferred_element_type=jnp.float32)


def conv_cube(padded, weights):
    kernel = weights.reshape(3, 3, 3, weights.shape[1], weights.shape[2]).transpose(2, 1, 0, 4, 3)
    result = lax.conv_general_dilated(
        padded[None], kernel, (1, 1, 1), "VALID",
        dimension_numbers=("NDHWC", "DHWIO", "NDHWC"), preferred_element_type=jnp.float32)
    return result[0]


def down_first(grid, weights):
    channels, size_z, size_y, size_x = grid.shape
    split = grid.reshape(channels, size_z // 2, 2, size_y // 2, 2, size_x // 2, 2)
    grouped = weights.reshape(2, 2, 2, weights.shape[1], weights.shape[2])
    return jnp.einsum("abkoi,izkybxa->zyxo", grouped, split, preferred_element_type=jnp.float32)


def down_cells(field, weights):
    size_z, size_y, size_x, channels = field.shape
    split = field.reshape(size_z // 2, 2, size_y // 2, 2, size_x // 2, 2, channels)
    grouped = weights.reshape(2, 2, 2, weights.shape[1], weights.shape[2])
    return jnp.einsum("abkoi,zkybxai->zyxo", grouped, split, preferred_element_type=jnp.float32)


def packed(field):
    size_z, size_y, size_x, chans = field.shape
    return field.transpose(3, 0, 1, 2).reshape(chans, size_z, size_y * size_x)


def local(volume, tissue, w_down1, b_down1, w_conv1a, b_conv1a, w_conv1b, b_conv1b,
          w_down2, b_down2, w_conv2a, b_conv2a, w_conv2b, b_conv2b):
    index_x = lax.axis_index("gx")
    index_y = lax.axis_index("gy")
    index_z = lax.axis_index("gz")
    grid_zero = volume.reshape(volume.shape[0], volume.shape[1], CY, CX)
    first_x = CX // 2
    first_y = CY // 2
    first_z = volume.shape[1] // 2
    first_blocks = (index_x * (first_x // 4), index_y * (first_y // 4), index_z * (first_z // 8))
    mask_one = region_mask(tissue, (4, 4, 8), first_blocks, (first_x, first_y, first_z), 0)
    mask_one_wide = region_mask(tissue, (4, 4, 8), first_blocks, (first_x, first_y, first_z), 1)
    down_one = finish(down_first(grid_zero, w_down1), b_down1, mask_one)
    inner_one = finish(conv_stacked(with_rim(down_one, 2, 0, True), w_conv1a), b_conv1a, mask_one_wide)
    feat_one = finish(conv_taps(inner_one, w_conv1b), b_conv1b, mask_one)
    second_x = first_x // 2
    second_y = first_y // 2
    second_z = first_z // 2
    second_blocks = (index_x * (second_x // 2), index_y * (second_y // 2), index_z * (second_z // 4))
    mask_two = region_mask(tissue, (2, 2, 4), second_blocks, (second_x, second_y, second_z), 0)
    mask_two_wide = region_mask(tissue, (2, 2, 4), second_blocks, (second_x, second_y, second_z), 1)
    down_two = finish(down_cells(feat_one, w_down2), b_down2, mask_two)
    middle = finish(conv_cube(rim_yxz(down_two, 2, 1), w_conv2a), b_conv2a, mask_two_wide)
    feat_two = finish(conv_cube(middle, w_conv2b), b_conv2b, mask_two)
    return (packed(feat_one), packed(feat_two))


def solution(mesh):
    return jax.shard_map(
        local,
        mesh=mesh,
        in_specs=(P(None, "gz", ("gx", "gy")),) + (P(),) * 13,
        out_specs=(P(None, "gz", ("gx", "gy")), P(None, "gz", ("gx", "gy"))),
        check_vma=False,
    )
```

```python
import functools

import jax
import jax.numpy as jnp
from jax import lax
from jax.experimental import pallas as pl
from jax.experimental.pallas import tpu as pltpu
from jax.sharding import PartitionSpec as P

CX = 64
CY = 32
AXES = ("gx", "gy", "gz")
MESH = pl.DeviceIdType.MESH
DIRS = [
    (dx, dy, dz)
    for dx in (-1, 0, 1)
    for dy in (-1, 0, 1)
    for dz in (-1, 0, 1)
    if (dx, dy, dz) != (0, 0, 0)
]


def rim_kernel(width, stack, f_ref, *refs):
    if stack:
        s_ref, p_ref, local_sem, send_sem, recv_sem = refs
    else:
        p_ref, local_sem, send_sem, recv_sem = refs
    size_z, size_y, size_x, _ = f_ref.shape
    sizes = (size_x, size_y, size_z)
    index = [lax.axis_index(a) for a in AXES]
    count = [lax.axis_size(a) for a in AXES]

    def exists(d):
        ok = True
        for a in range(3):
            if d[a] == -1:
                ok = jnp.logical_and(ok, index[a] > 0)
            elif d[a] == 1:
                ok = jnp.logical_and(ok, index[a] < count[a] - 1)
        return ok

    def device(d):
        return tuple(index[a] + d[a] for a in range(3))

    def source(a, step):
        s = sizes[a]
        if step == -1:
            return slice(0, width)
        if step == 1:
            return slice(s - width, s)
        return slice(0, s)

    def side(a, step):
        s = sizes[a]
        if step == -1:
            return slice(0, width)
        if step == 1:
            return slice(s + width, s + 2 * width)
        return slice(width, width + s)

    barrier = pltpu.get_barrier_semaphore()
    for d in DIRS:
        @pl.when(exists(d))
        def _():
            pl.semaphore_signal(barrier, inc=1, device_id=device(d), device_id_type=MESH)

    local = pltpu.make_async_copy(
        f_ref, p_ref.at[width:width + size_z, width:width + size_y, width:width + size_x, :],
        local_sem.at[0])
    local.start()

    for d in DIRS:
        @pl.when(jnp.logical_not(exists(d)))
        def _():
            sx, sy, sz = (side(a, d[a]) for a in range(3))
            region = p_ref.at[sz, sy, sx, :]
            region[...] = jnp.zeros(region.shape, region.dtype)

    peers = 1
    for a in range(3):
        below = (index[a] + count[a] - 1) // count[a]
        above = (2 * count[a] - 2 - index[a]) // count[a]
        peers = peers * (1 + below + above)
    pl.semaphore_wait(barrier, peers - 1)

    copies = []
    for k, d in enumerate(DIRS):
        sx, sy, sz = (source(a, d[a]) for a in range(3))
        tx, ty, tz = (side(a, -d[a]) for a in range(3))
        copy = pltpu.make_async_remote_copy(
            src_ref=f_ref.at[sz, sy, sx, :],
            dst_ref=p_ref.at[tz, ty, tx, :],
            send_sem=send_sem.at[k],
            recv_sem=recv_sem.at[k],
            device_id=device(d),
            device_id_type=MESH,
        )
        copies.append((d, copy))

        @pl.when(exists(d))
        def _():
            copy.start()

    local.wait()
    for d, copy in copies:
        @pl.when(exists(d))
        def _():
            copy.wait_send()

        @pl.when(exists(tuple(-v for v in d)))
        def _():
            copy.wait_recv()

    if stack:
        chans = f_ref.shape[3]
        depth = s_ref.shape[0]
        for k in range(3):
            s_ref[:, :, :, k * chans:(k + 1) * chans] = p_ref[k:k + depth]


def with_rim(field, width, collective_id, stack):
    size_z, size_y, size_x, chans = field.shape
    padded = (size_z + 2 * width, size_y + 2 * width, size_x + 2 * width, chans)
    sems = [
        pltpu.SemaphoreType.DMA((1,)),
        pltpu.SemaphoreType.DMA((len(DIRS),)),
        pltpu.SemaphoreType.DMA((len(DIRS),)),
    ]
    if stack:
        shape = (padded[0] - 2, padded[1], padded[2], 3 * chans)
        scratch = [pltpu.VMEM(padded, field.dtype)] + sems
    else:
        shape = padded
        scratch = sems
    return pl.pallas_call(
        functools.partial(rim_kernel, width, stack),
        out_shape=jax.ShapeDtypeStruct(shape, field.dtype),
        in_specs=[pl.BlockSpec(memory_space=pltpu.VMEM)],
        out_specs=pl.BlockSpec(memory_space=pltpu.VMEM),
        scratch_shapes=scratch,
        compiler_params=pltpu.CompilerParams(collective_id=collective_id, has_side_effects=True),
    )(field)


def conv_stacked(stacked, weights):
    kernel = weights.reshape(3, 3, 3, weights.shape[1], weights.shape[2]).transpose(1, 0, 2, 4, 3)
    kernel = kernel.reshape(3, 3, 3 * weights.shape[2], weights.shape[1])
    return lax.conv_general_dilated(
        stacked, kernel, (1, 1), "VALID",
        dimension_numbers=("NHWC", "HWIO", "NHWC"), preferred_element_type=jnp.float32)


def region_mask(tissue, repeats, block_starts, extents, margin):
    padded = jnp.pad(tissue, 1)
    counts = [extents[d] // repeats[d] + 2 for d in range(3)]
    starts = [jnp.asarray(block_starts[d], dtype=jnp.int32) for d in range(3)]
    table = lax.dynamic_slice(padded, starts, counts)
    for d in range(3):
        table = jnp.repeat(table, repeats[d], axis=d)
    table = table[
        repeats[0] - margin : repeats[0] + extents[0] + margin,
        repeats[1] - margin : repeats[1] + extents[1] + margin,
        repeats[2] - margin : repeats[2] + extents[2] + margin,
    ]
    return table.astype(jnp.float32).transpose(2, 1, 0)[..., None]


def finish(summed, offsets, tissue_mask):
    return (jnp.maximum(summed + offsets, 0.0) * tissue_mask).astype(jnp.bfloat16)


def conv_taps(padded, weights, out_spec="NHWC"):
    size_z = padded.shape[0] - 2
    stacked = jnp.concatenate([padded[k:k + size_z] for k in range(3)], axis=-1)
    kernel = weights.reshape(3, 3, 3, weights.shape[1], weights.shape[2]).transpose(1, 0, 2, 4, 3)
    kernel = kernel.reshape(3, 3, 3 * weights.shape[2], weights.shape[1])
    return lax.conv_general_dilated(
        stacked, kernel, (1, 1), "VALID",
        dimension_numbers=("NHWC", "HWIO", out_spec), preferred_element_type=jnp.float32)


def conv_cube(padded, weights):
    kernel = weights.reshape(3, 3, 3, weights.shape[1], weights.shape[2]).transpose(2, 1, 0, 4, 3)
    result = lax.conv_general_dilated(
        padded[None], kernel, (1, 1, 1), "VALID",
        dimension_numbers=("NDHWC", "DHWIO", "NDHWC"), preferred_element_type=jnp.float32)
    return result[0]


def down_first(grid, weights):
    channels, size_z, size_y, size_x = grid.shape
    split = grid.reshape(channels, size_z // 2, 2, size_y // 2, 2, size_x // 2, 2)
    grouped = weights.reshape(2, 2, 2, weights.shape[1], weights.shape[2])
    return jnp.einsum("abkoi,izkybxa->zyxo", grouped, split, preferred_element_type=jnp.float32)


def down_cells(field, weights):
    size_z, size_y, size_x, channels = field.shape
    split = field.reshape(size_z // 2, 2, size_y // 2, 2, size_x // 2, 2, channels)
    grouped = weights.reshape(2, 2, 2, weights.shape[1], weights.shape[2])
    return jnp.einsum("abkoi,zkybxai->zyxo", grouped, split, preferred_element_type=jnp.float32)


def packed(field):
    size_z, size_y, size_x, chans = field.shape
    return field.transpose(3, 0, 1, 2).reshape(chans, size_z, size_y * size_x)


def local(volume, tissue, w_down1, b_down1, w_conv1a, b_conv1a, w_conv1b, b_conv1b,
          w_down2, b_down2, w_conv2a, b_conv2a, w_conv2b, b_conv2b):
    index_x = lax.axis_index("gx")
    index_y = lax.axis_index("gy")
    index_z = lax.axis_index("gz")
    grid_zero = volume.reshape(volume.shape[0], volume.shape[1], CY, CX)
    first_x = CX // 2
    first_y = CY // 2
    first_z = volume.shape[1] // 2
    first_blocks = (index_x * (first_x // 4), index_y * (first_y // 4), index_z * (first_z // 8))
    mask_one = region_mask(tissue, (4, 4, 8), first_blocks, (first_x, first_y, first_z), 0)
    mask_one_wide = region_mask(tissue, (4, 4, 8), first_blocks, (first_x, first_y, first_z), 1)
    down_one = finish(down_first(grid_zero, w_down1), b_down1, mask_one)
    inner_one = finish(conv_stacked(with_rim(down_one, 2, 0, True), w_conv1a), b_conv1a, mask_one_wide)
    summed = conv_taps(inner_one, w_conv1b, "CNHW")
    feat_one = (jnp.maximum(summed + b_conv1b[:, None, None, None], 0.0) * mask_one[None, ..., 0]).astype(
        jnp.bfloat16)
    second_x = first_x // 2
    second_y = first_y // 2
    second_z = first_z // 2
    second_blocks = (index_x * (second_x // 2), index_y * (second_y // 2), index_z * (second_z // 4))
    mask_two = region_mask(tissue, (2, 2, 4), second_blocks, (second_x, second_y, second_z), 0)
    mask_two_wide = region_mask(tissue, (2, 2, 4), second_blocks, (second_x, second_y, second_z), 1)
    down_two = finish(down_first(feat_one, w_down2), b_down2, mask_two)
    middle = finish(conv_cube(with_rim(down_two, 2, 1, False), w_conv2a), b_conv2a, mask_two_wide)
    feat_two = finish(conv_cube(middle, w_conv2b), b_conv2b, mask_two)
    return (feat_one.reshape(feat_one.shape[0], feat_one.shape[1], -1), packed(feat_two))


def solution(mesh):
    return jax.shard_map(
        local,
        mesh=mesh,
        in_specs=(P(None, "gz", ("gx", "gy")),) + (P(),) * 13,
        out_specs=(P(None, "gz", ("gx", "gy")), P(None, "gz", ("gx", "gy"))),
        check_vma=False,
    )
```

```python
import functools

import jax
import jax.numpy as jnp
from jax import lax
from jax.experimental import pallas as pl
from jax.experimental.pallas import tpu as pltpu
from jax.sharding import PartitionSpec as P

CX = 64
CY = 32
AXES = ("gx", "gy", "gz")
MESH = pl.DeviceIdType.MESH
DIRS = [
    (dx, dy, dz)
    for dx in (-1, 0, 1)
    for dy in (-1, 0, 1)
    for dz in (-1, 0, 1)
    if (dx, dy, dz) != (0, 0, 0)
]
DIRS.sort(key=lambda d: sum(abs(v) for v in d))


def rim_kernel(width, stack, f_ref, *refs):
    if stack:
        s_ref, p_ref, local_sem, send_sem, recv_sem = refs
    else:
        p_ref, local_sem, send_sem, recv_sem = refs
    size_z, size_y, size_x, _ = f_ref.shape
    sizes = (size_x, size_y, size_z)
    index = [lax.axis_index(a) for a in AXES]
    count = [lax.axis_size(a) for a in AXES]

    def exists(d):
        ok = True
        for a in range(3):
            if d[a] == -1:
                ok = jnp.logical_and(ok, index[a] > 0)
            elif d[a] == 1:
                ok = jnp.logical_and(ok, index[a] < count[a] - 1)
        return ok

    def device(d):
        return tuple(index[a] + d[a] for a in range(3))

    def source(a, step):
        s = sizes[a]
        if step == -1:
            return slice(0, width)
        if step == 1:
            return slice(s - width, s)
        return slice(0, s)

    def side(a, step):
        s = sizes[a]
        if step == -1:
            return slice(0, width)
        if step == 1:
            return slice(s + width, s + 2 * width)
        return slice(width, width + s)

    barrier = pltpu.get_barrier_semaphore()
    for d in DIRS:
        @pl.when(exists(d))
        def _():
            pl.semaphore_signal(barrier, inc=1, device_id=device(d), device_id_type=MESH)

    local = pltpu.make_async_copy(
        f_ref, p_ref.at[width:width + size_z, width:width + size_y, width:width + size_x, :],
        local_sem.at[0])
    local.start()

    for d in DIRS:
        @pl.when(jnp.logical_not(exists(d)))
        def _():
            sx, sy, sz = (side(a, d[a]) for a in range(3))
            region = p_ref.at[sz, sy, sx, :]
            region[...] = jnp.zeros(region.shape, region.dtype)

    peers = 1
    for a in range(3):
        below = (index[a] + count[a] - 1) // count[a]
        above = (2 * count[a] - 2 - index[a]) // count[a]
        peers = peers * (1 + below + above)
    pl.semaphore_wait(barrier, peers - 1)

    copies = []
    for k, d in enumerate(DIRS):
        sx, sy, sz = (source(a, d[a]) for a in range(3))
        tx, ty, tz = (side(a, -d[a]) for a in range(3))
        copy = pltpu.make_async_remote_copy(
            src_ref=f_ref.at[sz, sy, sx, :],
            dst_ref=p_ref.at[tz, ty, tx, :],
            send_sem=send_sem.at[k],
            recv_sem=recv_sem.at[k],
            device_id=device(d),
            device_id_type=MESH,
        )
        copies.append((d, copy))

        @pl.when(exists(d))
        def _():
            copy.start()

    local.wait()
    for d, copy in copies:
        @pl.when(exists(d))
        def _():
            copy.wait_send()

        @pl.when(exists(tuple(-v for v in d)))
        def _():
            copy.wait_recv()

    if stack:
        chans = f_ref.shape[3]
        depth = s_ref.shape[0]
        for k in range(3):
            s_ref[:, :, :, k * chans:(k + 1) * chans] = p_ref[k:k + depth]


def with_rim(field, width, collective_id, stack):
    size_z, size_y, size_x, chans = field.shape
    padded = (size_z + 2 * width, size_y + 2 * width, size_x + 2 * width, chans)
    sems = [
        pltpu.SemaphoreType.DMA((1,)),
        pltpu.SemaphoreType.DMA((len(DIRS),)),
        pltpu.SemaphoreType.DMA((len(DIRS),)),
    ]
    if stack:
        shape = (padded[0] - 2, padded[1], padded[2], 3 * chans)
        scratch = [pltpu.VMEM(padded, field.dtype)] + sems
    else:
        shape = padded
        scratch = sems
    return pl.pallas_call(
        functools.partial(rim_kernel, width, stack),
        out_shape=jax.ShapeDtypeStruct(shape, field.dtype),
        in_specs=[pl.BlockSpec(memory_space=pltpu.VMEM)],
        out_specs=pl.BlockSpec(memory_space=pltpu.VMEM),
        scratch_shapes=scratch,
        compiler_params=pltpu.CompilerParams(collective_id=collective_id, has_side_effects=True),
    )(field)


def conv_stacked(stacked, weights):
    kernel = weights.reshape(3, 3, 3, weights.shape[1], weights.shape[2]).transpose(1, 0, 2, 4, 3)
    kernel = kernel.reshape(3, 3, 3 * weights.shape[2], weights.shape[1])
    return lax.conv_general_dilated(
        stacked, kernel, (1, 1), "VALID",
        dimension_numbers=("NHWC", "HWIO", "NHWC"), preferred_element_type=jnp.float32)


def region_mask(tissue, repeats, block_starts, extents, margin):
    padded = jnp.pad(tissue, 1)
    counts = [extents[d] // repeats[d] + 2 for d in range(3)]
    starts = [jnp.asarray(block_starts[d], dtype=jnp.int32) for d in range(3)]
    table = lax.dynamic_slice(padded, starts, counts)
    for d in range(3):
        table = jnp.repeat(table, repeats[d], axis=d)
    table = table[
        repeats[0] - margin : repeats[0] + extents[0] + margin,
        repeats[1] - margin : repeats[1] + extents[1] + margin,
        repeats[2] - margin : repeats[2] + extents[2] + margin,
    ]
    return table.astype(jnp.float32).transpose(2, 1, 0)[..., None]


def finish(summed, offsets, tissue_mask):
    return (jnp.maximum(summed + offsets, 0.0) * tissue_mask).astype(jnp.bfloat16)


def conv_taps(padded, weights):
    size_z = padded.shape[0] - 2
    stacked = jnp.concatenate([padded[k:k + size_z] for k in range(3)], axis=-1)
    kernel = weights.reshape(3, 3, 3, weights.shape[1], weights.shape[2]).transpose(1, 0, 2, 4, 3)
    kernel = kernel.reshape(3, 3, 3 * weights.shape[2], weights.shape[1])
    return lax.conv_general_dilated(
        stacked, kernel, (1, 1), "VALID",
        dimension_numbers=("NHWC", "HWIO", "NHWC"), preferred_element_type=jnp.float32)


def conv_cube(padded, weights):
    kernel = weights.reshape(3, 3, 3, weights.shape[1], weights.shape[2]).transpose(2, 1, 0, 4, 3)
    result = lax.conv_general_dilated(
        padded[None], kernel, (1, 1, 1), "VALID",
        dimension_numbers=("NDHWC", "DHWIO", "NDHWC"), preferred_element_type=jnp.float32)
    return result[0]


def down_first(grid, weights):
    channels, size_z, size_y, size_x = grid.shape
    split = grid.reshape(channels, size_z // 2, 2, size_y // 2, 2, size_x // 2, 2)
    grouped = weights.reshape(2, 2, 2, weights.shape[1], weights.shape[2])
    return jnp.einsum("abkoi,izkybxa->zyxo", grouped, split, preferred_element_type=jnp.float32)


def down_cells(field, weights):
    size_z, size_y, size_x, channels = field.shape
    split = field.reshape(size_z // 2, 2, size_y // 2, 2, size_x // 2, 2, channels)
    grouped = weights.reshape(2, 2, 2, weights.shape[1], weights.shape[2])
    return jnp.einsum("abkoi,zkybxai->zyxo", grouped, split, preferred_element_type=jnp.float32)


def packed(field):
    size_z, size_y, size_x, chans = field.shape
    return field.transpose(3, 0, 1, 2).reshape(chans, size_z, size_y * size_x)


def local(volume, tissue, w_down1, b_down1, w_conv1a, b_conv1a, w_conv1b, b_conv1b,
          w_down2, b_down2, w_conv2a, b_conv2a, w_conv2b, b_conv2b):
    index_x = lax.axis_index("gx")
    index_y = lax.axis_index("gy")
    index_z = lax.axis_index("gz")
    grid_zero = volume.reshape(volume.shape[0], volume.shape[1], CY, CX)
    first_x = CX // 2
    first_y = CY // 2
    first_z = volume.shape[1] // 2
    first_blocks = (index_x * (first_x // 4), index_y * (first_y // 4), index_z * (first_z // 8))
    mask_one = region_mask(tissue, (4, 4, 8), first_blocks, (first_x, first_y, first_z), 0)
    mask_one_wide = region_mask(tissue, (4, 4, 8), first_blocks, (first_x, first_y, first_z), 1)
    down_one = finish(down_first(grid_zero, w_down1), b_down1, mask_one)
    inner_one = finish(conv_stacked(with_rim(down_one, 2, 0, True), w_conv1a), b_conv1a, mask_one_wide)
    feat_one = finish(conv_taps(inner_one, w_conv1b), b_conv1b, mask_one)
    second_x = first_x // 2
    second_y = first_y // 2
    second_z = first_z // 2
    second_blocks = (index_x * (second_x // 2), index_y * (second_y // 2), index_z * (second_z // 4))
    mask_two = region_mask(tissue, (2, 2, 4), second_blocks, (second_x, second_y, second_z), 0)
    mask_two_wide = region_mask(tissue, (2, 2, 4), second_blocks, (second_x, second_y, second_z), 1)
    down_two = finish(down_cells(feat_one, w_down2), b_down2, mask_two)
    middle = finish(conv_cube(with_rim(down_two, 2, 1, False), w_conv2a), b_conv2a, mask_two_wide)
    feat_two = finish(conv_cube(middle, w_conv2b), b_conv2b, mask_two)
    return (packed(feat_one), packed(feat_two))


def solution(mesh):
    return jax.shard_map(
        local,
        mesh=mesh,
        in_specs=(P(None, "gz", ("gx", "gy")),) + (P(),) * 13,
        out_specs=(P(None, "gz", ("gx", "gy")), P(None, "gz", ("gx", "gy"))),
        check_vma=False,
    )
```

```python
import functools

import jax
import jax.numpy as jnp
from jax import lax
from jax.experimental import pallas as pl
from jax.experimental.pallas import tpu as pltpu
from jax.sharding import PartitionSpec as P

CX = 64
CY = 32
AXES = ("gx", "gy", "gz")
MESH = pl.DeviceIdType.MESH
DIRS = [
    (dx, dy, dz)
    for dx in (-1, 0, 1)
    for dy in (-1, 0, 1)
    for dz in (-1, 0, 1)
    if (dx, dy, dz) != (0, 0, 0)
]


def rim_kernel(width, stack, f_ref, *refs):
    if stack:
        s_ref, p_ref, local_sem, send_sem, recv_sem = refs
    else:
        p_ref, local_sem, send_sem, recv_sem = refs
    size_z, size_y, size_x, _ = f_ref.shape
    sizes = (size_x, size_y, size_z)
    index = [lax.axis_index(a) for a in AXES]
    count = [lax.axis_size(a) for a in AXES]

    def exists(d):
        ok = True
        for a in range(3):
            if d[a] == -1:
                ok = jnp.logical_and(ok, index[a] > 0)
            elif d[a] == 1:
                ok = jnp.logical_and(ok, index[a] < count[a] - 1)
        return ok

    def device(d):
        return tuple(index[a] + d[a] for a in range(3))

    def source(a, step):
        s = sizes[a]
        if step == -1:
            return slice(0, width)
        if step == 1:
            return slice(s - width, s)
        return slice(0, s)

    def side(a, step):
        s = sizes[a]
        if step == -1:
            return slice(0, width)
        if step == 1:
            return slice(s + width, s + 2 * width)
        return slice(width, width + s)

    barrier = pltpu.get_barrier_semaphore()
    for d in DIRS:
        @pl.when(exists(d))
        def _():
            pl.semaphore_signal(barrier, inc=1, device_id=device(d), device_id_type=MESH)

    local = pltpu.make_async_copy(
        f_ref, p_ref.at[width:width + size_z, width:width + size_y, width:width + size_x, :],
        local_sem.at[0])
    local.start()

    for d in DIRS:
        @pl.when(jnp.logical_not(exists(d)))
        def _():
            sx, sy, sz = (side(a, d[a]) for a in range(3))
            region = p_ref.at[sz, sy, sx, :]
            region[...] = jnp.zeros(region.shape, region.dtype)

    peers = 1
    for a in range(3):
        below = (index[a] + count[a] - 1) // count[a]
        above = (2 * count[a] - 2 - index[a]) // count[a]
        peers = peers * (1 + below + above)
    pl.semaphore_wait(barrier, peers - 1)

    copies = []
    for k, d in enumerate(DIRS):
        sx, sy, sz = (source(a, d[a]) for a in range(3))
        tx, ty, tz = (side(a, -d[a]) for a in range(3))
        copy = pltpu.make_async_remote_copy(
            src_ref=f_ref.at[sz, sy, sx, :],
            dst_ref=p_ref.at[tz, ty, tx, :],
            send_sem=send_sem.at[k],
            recv_sem=recv_sem.at[k],
            device_id=device(d),
            device_id_type=MESH,
        )
        copies.append((d, copy))

        @pl.when(exists(d))
        def _():
            copy.start()

    local.wait()
    for d, copy in copies:
        @pl.when(exists(d))
        def _():
            copy.wait_send()

        @pl.when(exists(tuple(-v for v in d)))
        def _():
            copy.wait_recv()

    if stack:
        chans = f_ref.shape[3]
        depth = s_ref.shape[0]
        for k in range(3):
            s_ref[:, :, :, k * chans:(k + 1) * chans] = p_ref[k:k + depth]


def with_rim(field, width, collective_id, stack):
    size_z, size_y, size_x, chans = field.shape
    padded = (size_z + 2 * width, size_y + 2 * width, size_x + 2 * width, chans)
    sems = [
        pltpu.SemaphoreType.DMA((1,)),
        pltpu.SemaphoreType.DMA((len(DIRS),)),
        pltpu.SemaphoreType.DMA((len(DIRS),)),
    ]
    if stack:
        shape = (padded[0] - 2, padded[1], padded[2], 3 * chans)
        scratch = [pltpu.VMEM(padded, field.dtype)] + sems
    else:
        shape = padded
        scratch = sems
    return pl.pallas_call(
        functools.partial(rim_kernel, width, stack),
        out_shape=jax.ShapeDtypeStruct(shape, field.dtype),
        in_specs=[pl.BlockSpec(memory_space=pltpu.VMEM)],
        out_specs=pl.BlockSpec(memory_space=pltpu.VMEM),
        scratch_shapes=scratch,
        compiler_params=pltpu.CompilerParams(collective_id=collective_id, has_side_effects=True),
    )(field)


def conv_stacked(stacked, weights):
    kernel = weights.reshape(3, 3, 3, weights.shape[1], weights.shape[2]).transpose(1, 0, 2, 4, 3)
    kernel = kernel.reshape(3, 3, 3 * weights.shape[2], weights.shape[1])
    return lax.conv_general_dilated(
        stacked, kernel, (1, 1), "VALID",
        dimension_numbers=("NHWC", "HWIO", "NHWC"), preferred_element_type=jnp.float32)


def region_mask(tissue, repeats, block_starts, extents, margin):
    padded = jnp.pad(tissue, 1)
    counts = [extents[d] // repeats[d] + 2 for d in range(3)]
    starts = [jnp.asarray(block_starts[d], dtype=jnp.int32) for d in range(3)]
    table = lax.dynamic_slice(padded, starts, counts)
    for d in range(3):
        table = jnp.repeat(table, repeats[d], axis=d)
    table = table[
        repeats[0] - margin : repeats[0] + extents[0] + margin,
        repeats[1] - margin : repeats[1] + extents[1] + margin,
        repeats[2] - margin : repeats[2] + extents[2] + margin,
    ]
    return table.astype(jnp.float32).transpose(2, 1, 0)[..., None]


def finish(summed, offsets, tissue_mask):
    return (jnp.maximum(summed + offsets, 0.0) * tissue_mask).astype(jnp.bfloat16)


def conv_taps(padded, weights):
    size_z = padded.shape[0] - 2
    stacked = jnp.concatenate([padded[k:k + size_z] for k in range(3)], axis=-1)
    kernel = weights.reshape(3, 3, 3, weights.shape[1], weights.shape[2]).transpose(1, 0, 2, 4, 3)
    kernel = kernel.reshape(3, 3, 3 * weights.shape[2], weights.shape[1])
    return lax.conv_general_dilated(
        stacked, kernel, (1, 1), "VALID",
        dimension_numbers=("NHWC", "HWIO", "NHWC"), preferred_element_type=jnp.float32)


def conv_cube(padded, weights):
    kernel = weights.reshape(3, 3, 3, weights.shape[1], weights.shape[2]).transpose(2, 1, 0, 4, 3)
    result = lax.conv_general_dilated(
        padded[None], kernel, (1, 1, 1), "VALID",
        dimension_numbers=("NDHWC", "DHWIO", "NDHWC"), preferred_element_type=jnp.float32)
    return result[0]


def down_first(grid, weights):
    channels, size_z, size_y, size_x = grid.shape
    split = grid.reshape(channels, size_z // 2, 2, size_y // 2, 2, size_x // 2, 2)
    grouped = weights.reshape(2, 2, 2, weights.shape[1], weights.shape[2])
    return jnp.einsum("abkoi,izkybxa->zyxo", grouped, split, preferred_element_type=jnp.float32)


def down_cells(field, weights):
    size_z, size_y, size_x, channels = field.shape
    split = field.reshape(size_z // 2, 2, size_y // 2, 2, size_x // 2, 2, channels)
    grouped = weights.reshape(2, 2, 2, weights.shape[1], weights.shape[2])
    return jnp.einsum("abkoi,zkybxai->zyxo", grouped, split, preferred_element_type=jnp.float32)


def packed(field):
    size_z, size_y, size_x, chans = field.shape
    return field.transpose(3, 0, 1, 2).reshape(chans, size_z, size_y * size_x)


def local(volume, tissue, w_down1, b_down1, w_conv1a, b_conv1a, w_conv1b, b_conv1b,
          w_down2, b_down2, w_conv2a, b_conv2a, w_conv2b, b_conv2b):
    index_x = lax.axis_index("gx")
    index_y = lax.axis_index("gy")
    index_z = lax.axis_index("gz")
    grid_zero = volume.reshape(volume.shape[0], volume.shape[1], CY, CX)
    first_x = CX // 2
    first_y = CY // 2
    first_z = volume.shape[1] // 2
    first_blocks = (index_x * (first_x // 4), index_y * (first_y // 4), index_z * (first_z // 8))
    mask_one_wide = region_mask(tissue, (4, 4, 8), first_blocks, (first_x, first_y, first_z), 1)
    mask_one = mask_one_wide[1:-1, 1:-1, 1:-1]
    down_one = finish(down_first(grid_zero, w_down1), b_down1, mask_one)
    inner_one = finish(conv_stacked(with_rim(down_one, 2, 0, True), w_conv1a), b_conv1a, mask_one_wide)
    feat_one = finish(conv_taps(inner_one, w_conv1b), b_conv1b, mask_one)
    second_x = first_x // 2
    second_y = first_y // 2
    second_z = first_z // 2
    second_blocks = (index_x * (second_x // 2), index_y * (second_y // 2), index_z * (second_z // 4))
    mask_two_wide = region_mask(tissue, (2, 2, 4), second_blocks, (second_x, second_y, second_z), 1)
    mask_two = mask_two_wide[1:-1, 1:-1, 1:-1]
    down_two = finish(down_cells(feat_one, w_down2), b_down2, mask_two)
    middle = finish(conv_cube(with_rim(down_two, 2, 1, False), w_conv2a), b_conv2a, mask_two_wide)
    feat_two = finish(conv_cube(middle, w_conv2b), b_conv2b, mask_two)
    return (packed(feat_one), packed(feat_two))


def solution(mesh):
    return jax.shard_map(
        local,
        mesh=mesh,
        in_specs=(P(None, "gz", ("gx", "gy")),) + (P(),) * 13,
        out_specs=(P(None, "gz", ("gx", "gy")), P(None, "gz", ("gx", "gy"))),
        check_vma=False,
    )
```
